32 devices in a mesh: basin: 4 (over x, core), tile: 8 (over z, y).
Axes of the slice: x: 2, y: 2, z: 4, core: 2. Of those that a mesh axis runs over, the one named last changes fastest.
Arguments:
- ocean_fields: bfloat16 [128, 24, 24, 256], P(('basin', 'tile')), may hold values from -6 to 6
- slot_tiles: int32 [128], P(('basin', 'tile')), may hold values from -1 to 31, as said below
- side_sources: int32 [128, 4], P(('basin', 'tile')), may hold values from -1 to 31, as said below
- corner_sources: int32 [128, 4], P(('basin', 'tile')), may hold values from -1 to 31, as said below
- side_sends: int32 [32, 8, 2], P(('basin', 'tile')), may hold values from -1 to 15, as said below
- corner_sends: int32 [32, 8, 2], P(('basin', 'tile')), may hold values from -1 to 15, as said below
- depth_kernel: bfloat16 [49, 256], replicated, may hold values from -0.875 to 0.875
- expand_weight: bfloat16 [256, 1024], replicated, may hold values from -0.375 to 0.375
- reduce_weight: bfloat16 [1024, 256], replicated, may hold values from -0.1875 to 0.1875
- field_cotangent: bfloat16 [128, 24, 24, 256], P(('basin', 'tile')), may hold values from -6 to 6
Outputs:
- next_fields: bfloat16 [128, 24, 24, 256], P(('basin', 'tile'))
- field_grad: bfloat16 [128, 24, 24, 256], P(('basin', 'tile'))
- kernel_grad: float32 [49, 256], replicated
- expand_grad: float32 [256, 1024], replicated
- reduce_grad: float32 [1024, 256], replicated
The draws below stay inside these ranges and needn't reach their ends.
Inputs may be any that keep to these rules, and one draw needn't show every extreme that they name: `slot_tiles`: each ocean position of a basin is named by exactly one slot of that basin's devices and land positions by none; -1 marks an empty slot. In every basin some device has all 4 slots filled. `side_sources`: an entry is -1 where the neighbouring position is land or beyond the band's first or last tile row; otherwise it names the neighbour's edge record that faces the slot, the band closing in longitude. Slots that are empty have -1 everywhere. `corner_sources`: as side_sources, for the diagonal neighbours and the corner that faces the slot. `side_sends`: [device, peer, k] is the own edge record that is the k-th record for that peer of the same basin, or -1; each record sent is read by exactly one entry of the peer's side_sources, and every such entry is sent. No device sends to itself. In every basin some pair of devices uses all 2 positions. `corner_sends`: as side_sends, for the corner records and corner_sources.
All inputs are finite; a program needn't handle non-finite values.
Results may differ from the reference program's by a relative error of at most 0.006.
Values may be sent and summed in bfloat16 or wider, within the bound.
No kernel may reach another device: no remote copies, remote signals or barrier semaphores. Data moves between devices by JAX's collectives and lax.ppermute only.
A program may use at most 128 MiB of HBM per device.

```python
import math
from functools import partial
import jax
import jax.numpy as jnp
from jax import lax

CHANNELS = 256
HIDDEN_SIZE = 1024
KERNEL = 7
TILE_EDGE = 24
TILE_SLOTS = 4
CAPACITY = 2
GRID_ROWS = 4
HALO_WIDTH = 3
GRID_COLS = 8
ALL_SLOTS = 128
ALL_CELLS = 73728
N_BASIN = 4


side_moves = ((-1, 0), (1, 0), (0, -1), (0, 1))


side_pieces = (1, 0, 3, 2)


corner_moves = ((-1, -1), (-1, 1), (1, -1), (1, 1))


corner_pieces = (3, 2, 1, 0)


def link_tables(moves, pieces, ocean_mask, device, slot_index, row_ids, col_ids):
    usable_list = []
    source_list = []
    target_list = []
    piece_list = []
    slot_list = []
    direction_list = []
    for direction in range(4):
        near_row = row_ids + moves[direction][0]
        near_col = (col_ids + moves[direction][1]) % GRID_COLS
        safe_row = jnp.clip(near_row, 0, GRID_ROWS - 1)
        inside = (near_row >= 0) & (near_row < GRID_ROWS)
        usable_list.append((ocean_mask & inside & ocean_mask[safe_row, near_col]).reshape(-1))
        source_list.append(device[safe_row, near_col].reshape(-1))
        target_list.append(device.reshape(-1))
        piece_list.append((slot_index[safe_row, near_col] * 4 + pieces[direction]).reshape(-1))
        slot_list.append((device * TILE_SLOTS + slot_index).reshape(-1))
        direction_list.append(jnp.full((GRID_ROWS * GRID_COLS,), direction, jnp.int32))
    usable = jnp.concatenate(usable_list)
    source_device = jnp.concatenate(source_list)
    target_device = jnp.concatenate(target_list)
    piece_code = jnp.concatenate(piece_list)
    target_slot = jnp.concatenate(slot_list)
    direction_ids = jnp.concatenate(direction_list)
    remote = usable & (source_device != target_device)
    pair_ids = source_device * GRID_COLS + target_device
    entry_ids = jnp.arange(pair_ids.shape[0])
    earlier = entry_ids[None, :] < entry_ids[:, None]
    same_pair = (pair_ids[:, None] == pair_ids[None, :]) & remote[None, :] & earlier
    slot_rank = jnp.sum(same_pair.astype(jnp.int32), axis=1).astype(jnp.int32)
    recv_code = jnp.where(usable, jnp.where(remote, source_device * CAPACITY + slot_rank, GRID_COLS * CAPACITY + piece_code), -1).astype(jnp.int32)
    sources = jnp.full((GRID_COLS * TILE_SLOTS, 4), -1, jnp.int32).at[target_slot, direction_ids].set(recv_code)
    sender = jnp.where(remote, source_device, GRID_COLS)
    send_table = jnp.full((GRID_COLS, GRID_COLS, CAPACITY), -1, jnp.int32).at[sender, target_device, slot_rank].set(piece_code.astype(jnp.int32), mode='drop')
    return (sources, send_table)


def basin_layout(basin_key):
    owner_key, slot_key, ocean_key, forced_key = jax.random.split(basin_key, 4)
    square_cols = GRID_COLS // 2
    square_owner = jax.random.permutation(owner_key, GRID_COLS).astype(jnp.int32)
    slot_order = jax.vmap(lambda one_key: jax.random.permutation(one_key, TILE_SLOTS))(jax.random.split(slot_key, GRID_COLS)).astype(jnp.int32)
    row_ids = jnp.arange(GRID_ROWS, dtype=jnp.int32)[:, None] * jnp.ones((1, GRID_COLS), jnp.int32)
    col_ids = jnp.ones((GRID_ROWS, 1), jnp.int32) * jnp.arange(GRID_COLS, dtype=jnp.int32)[None, :]
    forced = jax.random.randint(forced_key, (), 0, square_cols)
    ocean_mask = (jax.random.randint(ocean_key, (GRID_ROWS, GRID_COLS), 0, 5) < 3) | (col_ids // 2 == forced)
    square = row_ids // 2 * square_cols + col_ids // 2
    within = row_ids % 2 * 2 + col_ids % 2
    device = square_owner[square]
    slot_index = slot_order[square, within]
    location = device * TILE_SLOTS + slot_index
    held = jnp.where(ocean_mask, row_ids * GRID_COLS + col_ids, -1).astype(jnp.int32)
    slot_tiles = jnp.full((GRID_COLS * TILE_SLOTS,), -1, jnp.int32).at[location.reshape(-1)].set(held.reshape(-1))
    side_src, side_table = link_tables(side_moves, side_pieces, ocean_mask, device, slot_index, row_ids, col_ids)
    corner_src, corner_table = link_tables(corner_moves, corner_pieces, ocean_mask, device, slot_index, row_ids, col_ids)
    return (slot_tiles, side_src, corner_src, side_table, corner_table)


def band_layout(key):
    basin_keys = jax.random.split(jax.random.fold_in(key, 17), N_BASIN)
    return jax.vmap(basin_layout)(basin_keys)


def draw_slot_tiles(key, part):
    return band_layout(key)[0].reshape(N_BASIN * GRID_COLS * TILE_SLOTS)


def draw_side_sources(key, part):
    return band_layout(key)[1].reshape(N_BASIN * GRID_COLS * TILE_SLOTS, 4)


def draw_corner_sources(key, part):
    return band_layout(key)[2].reshape(N_BASIN * GRID_COLS * TILE_SLOTS, 4)


def draw_side_sends(key, part):
    return band_layout(key)[3].reshape(N_BASIN * GRID_COLS, GRID_COLS, CAPACITY)


def draw_corner_sends(key, part):
    return band_layout(key)[4].reshape(N_BASIN * GRID_COLS, GRID_COLS, CAPACITY)


def block_scale(rng, dims, shards, least, high):
    gain, own = 1.0, jax.random.fold_in(rng, 6)
    for axis_at, shards_of in shards:
        steps = jnp.exp(jax.random.uniform(jax.random.fold_in(own, axis_at), (shards_of,), jnp.float32, least / len(shards), high / len(shards)))
        gain = gain * jnp.repeat(steps, dims[axis_at] // shards_of).reshape([-1 if axis == axis_at else 1 for axis in range(len(dims))])
    return gain


def gaussian(rng, extent, scale, limit, cuts=(), held_as=jnp.bfloat16):
    result = scale * jax.random.normal(rng, extent, jnp.float32)
    if cuts:
        result = result * block_scale(rng, extent, cuts, -0.22, 0.18)
    return jnp.clip(result, -limit, limit).astype(held_as)


def setup_inputs(seed: int = 0) -> dict:
    key_list = jax.random.split(jax.random.key(seed), 11)
    ocean_fields = gaussian(key_list[0], (ALL_SLOTS, TILE_EDGE, TILE_EDGE, CHANNELS), 1.0, 6.0, ((0, 32),))
    slot_tiles = draw_slot_tiles(jax.random.fold_in(key_list[10], 71), 0)
    side_sources = draw_side_sources(jax.random.fold_in(key_list[10], 71), 0)
    corner_sources = draw_corner_sources(jax.random.fold_in(key_list[10], 71), 0)
    side_sends = draw_side_sends(jax.random.fold_in(key_list[10], 71), 0)
    corner_sends = draw_corner_sends(jax.random.fold_in(key_list[10], 71), 0)
    depth_kernel = gaussian(key_list[6], (KERNEL * KERNEL, CHANNELS), (KERNEL * KERNEL) ** -0.5, 0.875)
    expand_weight = gaussian(key_list[7], (CHANNELS, HIDDEN_SIZE), CHANNELS ** -0.5, 0.375)
    reduce_weight = gaussian(key_list[8], (HIDDEN_SIZE, CHANNELS), HIDDEN_SIZE ** -0.5, 0.1875)
    field_cotangent = gaussian(key_list[9], (ALL_SLOTS, TILE_EDGE, TILE_EDGE, CHANNELS), 1.0, 6.0, ((0, 32),))
    return dict(ocean_fields=ocean_fields, slot_tiles=slot_tiles, side_sources=side_sources, corner_sources=corner_sources, side_sends=side_sends, corner_sends=corner_sends, depth_kernel=depth_kernel, expand_weight=expand_weight, reduce_weight=reduce_weight, field_cotangent=field_cotangent)


ln_eps = 1e-06

def gelu_parts(pre_act):
    normal_cdf = 0.5 * (1.0 + jax.scipy.special.erf(pre_act * (1.0 / math.sqrt(2.0))))
    density = jnp.exp(-0.5 * pre_act * pre_act) * (1.0 / math.sqrt(2.0 * math.pi))
    return (pre_act * normal_cdf, normal_cdf + pre_act * density)

def edge_pieces(tile_data):
    rim_size = HALO_WIDTH
    slot_count = tile_data.shape[0]
    side_rows = jnp.stack([tile_data[:, :rim_size], tile_data[:, -rim_size:], jnp.swapaxes(tile_data[:, :, :rim_size], 1, 2), jnp.swapaxes(tile_data[:, :, -rim_size:], 1, 2)], axis=1)
    corner_rows = jnp.stack([tile_data[:, :rim_size, :rim_size], tile_data[:, :rim_size, -rim_size:], tile_data[:, -rim_size:, :rim_size], tile_data[:, -rim_size:, -rim_size:]], axis=1)
    return (side_rows.reshape((slot_count * 4,) + side_rows.shape[2:]), corner_rows.reshape((slot_count * 4,) + corner_rows.shape[2:]))

def resolve(flat_own, sources, sends):
    own_count = TILE_SLOTS * 4
    remote_count = GRID_COLS * CAPACITY
    codes = sources.reshape(GRID_COLS, TILE_SLOTS, 4).astype(jnp.int32)
    receiver = jnp.arange(GRID_COLS, dtype=jnp.int32)[:, None, None] * jnp.ones((1, TILE_SLOTS, 4), jnp.int32)
    safe_codes = jnp.clip(codes, 0, remote_count + own_count - 1).astype(jnp.int32)
    remote = codes < remote_count
    sender = jnp.where(remote, jnp.clip(safe_codes // CAPACITY, 0, GRID_COLS - 1), receiver).astype(jnp.int32)
    position = (safe_codes % CAPACITY).astype(jnp.int32)
    sent = sends[sender, receiver, position].astype(jnp.int32)
    record = jnp.where(remote, sent, safe_codes - remote_count).astype(jnp.int32)
    valid = (codes >= 0) & (record >= 0)
    index = jnp.clip(sender * own_count + record, 0, GRID_COLS * own_count - 1).astype(jnp.int32)
    picked = jnp.take(flat_own, index.reshape(-1), axis=0)
    keep_mask = valid.reshape((-1,) + (1,) * (flat_own.ndim - 1))
    picked = jnp.where(keep_mask, picked, jnp.zeros_like(picked))
    return picked.reshape((GRID_COLS * TILE_SLOTS, 4) + flat_own.shape[1:])

def pad_by_lists(tile_data, side_sources, corner_sources, side_sends, corner_sends):
    side_own, corner_own = edge_pieces(tile_data)
    side_halo = resolve(side_own, side_sources, side_sends)
    corner_halo = resolve(corner_own, corner_sources, corner_sends)
    top_band = jnp.concatenate([corner_halo[:, 0], side_halo[:, 0], corner_halo[:, 1]], axis=2)
    middle = jnp.concatenate([jnp.swapaxes(side_halo[:, 2], 1, 2), tile_data, jnp.swapaxes(side_halo[:, 3], 1, 2)], axis=2)
    bottom_band = jnp.concatenate([corner_halo[:, 2], side_halo[:, 1], corner_halo[:, 3]], axis=2)
    return jnp.concatenate([top_band, middle, bottom_band], axis=1)

def depthwise(padded, kernel, out_edge):
    summed = jnp.zeros((padded.shape[0], out_edge, out_edge, padded.shape[-1]), jnp.float32)
    for row_off in range(KERNEL):
        for col_off in range(KERNEL):
            weight_row = kernel[row_off * KERNEL + col_off].astype(jnp.float32)
            window = padded[:, row_off:row_off + out_edge, col_off:col_off + out_edge]
            summed = summed + window.astype(jnp.float32) * weight_row
    return summed

def tile_step(expand_weight, reduce_weight, carry, item):
    expand_acc, reduce_acc = carry
    mixed_rows, cot_rows = item
    centre = mixed_rows - lax.optimization_barrier(jnp.mean(mixed_rows, axis=1, keepdims=True))
    scale_inv = lax.rsqrt(lax.optimization_barrier(jnp.mean(centre * centre, axis=1, keepdims=True)) + ln_eps)
    unit_rows = centre * scale_inv
    normed = unit_rows.astype(jnp.bfloat16)
    pre_act = jnp.dot(normed, expand_weight, preferred_element_type=jnp.float32)
    act_value, act_slope = gelu_parts(pre_act)
    activated = act_value.astype(jnp.bfloat16)
    update = jnp.dot(activated, reduce_weight, preferred_element_type=jnp.float32)
    grad_act = jnp.dot(cot_rows, reduce_weight.T, preferred_element_type=jnp.float32)
    grad_pre = (grad_act * act_slope).astype(jnp.bfloat16)
    reduce_acc = reduce_acc + jnp.dot(activated.T, cot_rows, preferred_element_type=jnp.float32)
    expand_acc = expand_acc + jnp.dot(normed.T, grad_pre, preferred_element_type=jnp.float32)
    grad_norm = jnp.dot(grad_pre, expand_weight.T, preferred_element_type=jnp.float32)
    grad_mixed = scale_inv * (grad_norm - lax.optimization_barrier(jnp.mean(grad_norm, axis=1, keepdims=True)) - unit_rows * lax.optimization_barrier(jnp.mean(grad_norm * unit_rows, axis=1, keepdims=True)))
    return ((expand_acc, reduce_acc), (update, grad_mixed.astype(jnp.bfloat16)))

def reference(ocean_fields, slot_tiles, side_sources, corner_sources, side_sends, corner_sends, depth_kernel, expand_weight, reduce_weight, field_cotangent):
    per_basin = GRID_COLS * TILE_SLOTS
    tile_cells = TILE_EDGE * TILE_EDGE
    flipped = depth_kernel.reshape(KERNEL, KERNEL, CHANNELS)[::-1, ::-1].reshape(KERNEL * KERNEL, CHANNELS)
    kernel_sum = jnp.zeros((KERNEL * KERNEL, CHANNELS), jnp.float32)
    expand_sum = jnp.zeros((CHANNELS, HIDDEN_SIZE), jnp.float32)
    reduce_sum = jnp.zeros((HIDDEN_SIZE, CHANNELS), jnp.float32)
    next_parts = []
    grad_parts = []
    for basin_index in range(N_BASIN):
        first = basin_index * per_basin
        dev_first = basin_index * GRID_COLS
        live_mask = (slot_tiles[first:first + per_basin] >= 0)[:, None, None, None]
        side_src = side_sources[first:first + per_basin]
        corner_src = corner_sources[first:first + per_basin]
        side_tab = side_sends[dev_first:dev_first + GRID_COLS]
        corner_tab = corner_sends[dev_first:dev_first + GRID_COLS]
        fields = ocean_fields[first:first + per_basin]
        fields = jnp.where(live_mask, fields, jnp.zeros_like(fields))
        cotangent = field_cotangent[first:first + per_basin]
        cotangent = jnp.where(live_mask, cotangent, jnp.zeros_like(cotangent))
        padded = pad_by_lists(fields, side_src, corner_src, side_tab, corner_tab)
        mixed = depthwise(padded, depth_kernel, TILE_EDGE)
        mixed_rows = mixed.reshape(per_basin, tile_cells, CHANNELS)
        cot_rows = cotangent.reshape(per_basin, tile_cells, CHANNELS)
        carry_init = (jnp.zeros((CHANNELS, HIDDEN_SIZE), jnp.float32), jnp.zeros((HIDDEN_SIZE, CHANNELS), jnp.float32))
        (expand_part, reduce_part), (updates, grad_mixed) = lax.scan(partial(tile_step, expand_weight, reduce_weight), carry_init, (mixed_rows, cot_rows))
        expand_sum = expand_sum + expand_part
        reduce_sum = reduce_sum + reduce_part
        next_slots = (fields.astype(jnp.float32) + updates.reshape(fields.shape)).astype(jnp.bfloat16)
        grad_tiles = grad_mixed.reshape(fields.shape)
        grad_padded = pad_by_lists(grad_tiles, side_src, corner_src, side_tab, corner_tab)
        spread = depthwise(grad_padded, flipped, TILE_EDGE)
        grad_slots = (cotangent.astype(jnp.float32) + spread).astype(jnp.bfloat16)
        grad_f = grad_tiles.astype(jnp.float32)
        kernel_terms = []
        for row_off in range(KERNEL):
            for col_off in range(KERNEL):
                window = padded[:, row_off:row_off + TILE_EDGE, col_off:col_off + TILE_EDGE].astype(jnp.float32)
                kernel_terms.append(lax.optimization_barrier(jnp.sum(grad_f * window, axis=(0, 1, 2))))
        kernel_sum = kernel_sum + jnp.stack(kernel_terms)
        next_parts.append(jnp.where(live_mask, next_slots, jnp.zeros_like(next_slots)))
        grad_parts.append(jnp.where(live_mask, grad_slots, jnp.zeros_like(grad_slots)))
    factor = 1.0 / math.sqrt(ALL_CELLS)
    next_fields = jnp.concatenate(next_parts, axis=0)
    field_grad = jnp.concatenate(grad_parts, axis=0)
    return (next_fields, field_grad, kernel_sum * factor, expand_sum * factor, reduce_sum * factor)
```

```python
import functools
import math

import jax
import jax.numpy as jnp
from jax import lax
from jax.experimental import pallas as pl
from jax.experimental.pallas import tpu as pltpu
from jax.sharding import PartitionSpec as P

KERNEL = 7
TAPS = KERNEL * KERNEL
RIM = 3
LANES = 128
COL0 = 8
LN_EPS = 1e-06
F32 = jnp.float32
BF16 = jnp.bfloat16
VMEM_LIMIT = 60 * 1024 * 1024


def mxu(lhs, rhs, lhs_dim, rhs_dim):
    return lax.dot_general(
        lhs, rhs, (((lhs_dim,), (rhs_dim,)), ((), ())), preferred_element_type=F32
    )


def gelu_parts(pre):
    cdf = 0.5 * (1.0 + lax.erf(pre * (1.0 / math.sqrt(2.0))))
    density = jnp.exp(-0.5 * pre * pre) * (1.0 / math.sqrt(2.0 * math.pi))
    return pre * cdf, cdf + pre * density


def live_factor(slot_ref, slot):
    return jnp.where(slot_ref[slot] >= 0, 1.0, 0.0).astype(F32)


def own_records(cells, side, corner, base, edge, slots):
    area = edge * edge
    rim_rows = RIM * edge
    far = edge - RIM
    for grp in range(cells.shape[0]):
        for s in range(slots):
            at = base + 4 * s
            start = s * area
            side[at, grp] = cells[grp, start : start + rim_rows]
            side[at + 1, grp] = cells[grp, start + area - rim_rows : start + area]
            for c in range(RIM):
                rows = slice(c * edge, (c + 1) * edge)
                side[at + 2, grp, rows] = cells[grp, pl.ds(start + c, edge, stride=edge)]
                side[at + 3, grp, rows] = cells[grp, pl.ds(start + far + c, edge, stride=edge)]
            for e in range(4):
                row0 = far if e // 2 else 0
                col0 = far if e % 2 else 0
                for r in range(RIM):
                    first = start + (row0 + r) * edge + col0
                    corner[at + e, grp, RIM * r : RIM * r + RIM] = cells[grp, first : first + RIM]


def send_records(send, side, corner, side_sends, corner_sends, zero_at):
    peers = send.shape[0]
    groups = side.shape[1]
    cap = side_sends.shape[0] // peers

    def one_peer(p, carry):
        for grp in range(groups):
            pieces = []
            for table, sends in ((side, side_sends), (corner, corner_sends)):
                for k in range(cap):
                    code = sends[p * cap + k]
                    pieces.append(table[jnp.where(code < 0, zero_at, code), grp])
            block = jnp.concatenate(pieces, axis=0)
            send[p, :, grp * LANES : (grp + 1) * LANES] = block.astype(BF16)
        return carry

    lax.fori_loop(0, peers, one_peer, 0)


def received_records(recv, side, corner, cap):
    groups = side.shape[1]
    n_side = side.shape[2]
    n_corner = corner.shape[2]

    def one_peer(p, carry):
        for grp in range(groups):
            block = recv[p, :, grp * LANES : (grp + 1) * LANES].astype(F32)
            for k in range(cap):
                side[p * cap + k, grp] = block[k * n_side : (k + 1) * n_side]
                first = cap * n_side + k * n_corner
                corner[p * cap + k, grp] = block[first : first + n_corner]
        return carry

    lax.fori_loop(0, recv.shape[0], one_peer, 0)


def place_rim(padded, side, corner, side_sources, corner_sources, slot, zero_at, edge):
    for e in range(4):
        code = side_sources[slot * 4 + e]
        at = jnp.where(code < 0, zero_at, code)
        for grp in range(side.shape[1]):
            for c in range(RIM):
                piece = side[at, grp, c * edge : (c + 1) * edge]
                if e < 2:
                    row = c if e == 0 else RIM + edge + c
                    padded[grp, row, COL0 : COL0 + edge] = piece
                else:
                    col = COL0 - RIM + c if e == 2 else COL0 + edge + c
                    padded[grp, RIM : RIM + edge, col] = piece
        code = corner_sources[slot * 4 + e]
        at = jnp.where(code < 0, zero_at, code)
        row0 = RIM + edge if e // 2 else 0
        col0 = COL0 + edge if e % 2 else COL0 - RIM
        for grp in range(side.shape[1]):
            for r in range(RIM):
                padded[grp, row0 + r, col0 : col0 + RIM] = corner[
                    at, grp, RIM * r : RIM * r + RIM
                ]


def spread_taps(taps, kernel_ref):
    for grp in range(taps.shape[0]):
        for t in range(TAPS):
            row = kernel_ref[t : t + 1, grp * LANES : (grp + 1) * LANES].astype(F32)
            taps[grp, t] = jnp.broadcast_to(row, taps.shape[2:])


def conv_group(padded, taps, grp, edge, part, flipped, emit):
    blocks = edge // 8
    lane = lax.broadcasted_iota(jnp.int32, (8, LANES), 0)
    for blk in range(blocks):
        acc = [None] * edge
        for b in range(KERNEL):
            west = part == "rim" and blk == 0 and b < RIM
            east = part == "rim" and blk == blocks - 1 and b > RIM
            weights = []
            for a in range(KERNEL):
                t = a * KERNEL + b
                weights.append(taps[grp, TAPS - 1 - t if flipped else t])
            for r in range(edge + 2 * RIM):
                inner = RIM <= r < RIM + edge
                if part == "own" and not inner:
                    continue
                if part == "rim" and inner and not (west or east):
                    continue
                first = COL0 - RIM + b + 8 * blk
                cells = padded[grp, r, first : first + 8]
                if part == "rim" and inner:
                    keep = lane < RIM - b if west else lane >= 8 + RIM - b
                    cells = jnp.where(keep, cells, 0.0)
                for a in range(KERNEL):
                    row = r - a
                    if 0 <= row < edge:
                        term = cells * weights[a]
                        acc[row] = term if acc[row] is None else acc[row] + term
        for row in range(edge):
            emit(blk, row, acc[row])


def kernel_grad_group(padded, grad, sums, grp, edge):
    for b in range(KERNEL):
        acc = [None] * KERNEL
        for blk in range(edge // 8):
            rows = [grad[grp, RIM + i, COL0 + 8 * blk : COL0 + 8 * blk + 8] for i in range(edge)]
            for r in range(edge + 2 * RIM):
                first = COL0 - RIM + b + 8 * blk
                cells = padded[0, grp, r, first : first + 8]
                for a in range(KERNEL):
                    if 0 <= r - a < edge:
                        term = rows[r - a] * cells
                        acc[a] = term if acc[a] is None else acc[a] + term
        for a in range(KERNEL):
            sums[grp, a * KERNEL + b] += acc[a]


def pack_body(slot_ref, side_sends, corner_sends, field, send, cells, side, corner, *, edge):
    slots = field.shape[0]
    own = 4 * slots
    area = edge * edge
    for s in range(slots):
        factor = live_factor(slot_ref, s)
        for grp in range(cells.shape[0]):
            for i in list(range(edge)):
                row = field[s, i, :, grp * LANES : (grp + 1) * LANES].astype(F32)
                first = s * area + i * edge
                cells[grp, first : first + edge] = row * factor
    side[own] = jnp.zeros(side.shape[1:], F32)
    corner[...] = jnp.zeros_like(corner)
    own_records(cells, side, corner, 0, edge, slots)
    send_records(send, side, corner, side_sends, corner_sends, own)


def own_body(slot_ref, field, kernel_ref, mixed, padded, taps, *, edge):
    s = pl.program_id(0)
    groups = padded.shape[0]

    @pl.when(s == 0)
    def _():
        padded[...] = jnp.zeros_like(padded)
        spread_taps(taps, kernel_ref)

    factor = live_factor(slot_ref, s)
    for grp in range(groups):
        for i in range(edge):
            row = field[0, i, :, grp * LANES : (grp + 1) * LANES].astype(F32)
            padded[grp, RIM + i, COL0 : COL0 + edge] = row * factor

    def one_group(grp, carry):
        def emit(blk, row, total):
            mixed[0, grp, row, 8 * blk : 8 * blk + 8] = total

        conv_group(padded, taps, grp, edge, "own", False, emit)
        return carry

    lax.fori_loop(0, groups, one_group, 0)


def forward_body(
    slot_ref,
    side_sources,
    corner_sources,
    recv,
    field,
    mixed_own,
    cotangent,
    kernel_ref,
    expand,
    reduce,
    out,
    padded_out,
    unit_out,
    scale_out,
    slope_out,
    reduce_out,
    side,
    corner,
    cells,
    taps,
    mixed,
    reduce_sum,
    *,
    edge,
    cap,
):
    s = pl.program_id(0)
    slots = pl.num_programs(0)
    groups = taps.shape[0]
    area = edge * edge
    n_slots = field.shape[0]
    base = recv.shape[0] * cap
    zero_at = base + 4 * n_slots
    hidden = expand.shape[1]

    @pl.when(s == 0)
    def _():
        for t in range(n_slots):
            factor = live_factor(slot_ref, t)
            for grp in range(groups):
                for i in range(edge):
                    row = field[t, i, :, grp * LANES : (grp + 1) * LANES].astype(F32)
                    first = t * area + i * edge
                    cells[grp, first : first + edge] = row * factor
        side[zero_at] = jnp.zeros(side.shape[1:], F32)
        corner[zero_at] = jnp.zeros(corner.shape[1:], F32)
        received_records(recv, side, corner, cap)
        own_records(cells, side, corner, base, edge, n_slots)
        spread_taps(taps, kernel_ref)
        reduce_sum[...] = jnp.zeros_like(reduce_sum)

    padded = padded_out.at[0]
    for grp in range(groups):
        for i in range(edge):
            first = pl.multiple_of(s * area + i * edge, 8)
            padded[grp, RIM + i, COL0 : COL0 + edge] = cells[grp, pl.ds(first, edge)]
    place_rim(padded, side, corner, side_sources, corner_sources, s, zero_at, edge)

    def one_group(grp, carry):
        def emit(blk, row, total):
            own = mixed_own[0, grp, row, 8 * blk : 8 * blk + 8]
            first = row * edge + 8 * blk
            mixed[grp, first : first + 8] = own if total is None else own + total

        conv_group(padded, taps, grp, edge, "rim", False, emit)
        return carry

    lax.fori_loop(0, groups, one_group, 0)

    channels = groups * LANES
    parts = [mixed[grp] for grp in range(groups)]
    mean = sum(jnp.sum(part, axis=1, keepdims=True) for part in parts) * (1.0 / channels)
    parts = [part - mean for part in parts]
    var = sum(jnp.sum(part * part, axis=1, keepdims=True) for part in parts) * (1.0 / channels)
    scale = lax.rsqrt(var + LN_EPS)
    unit = jnp.concatenate([part * scale for part in parts], axis=1)
    unit_out[...] = unit
    scale_out[...] = scale
    normed = unit.astype(BF16)
    cot = cotangent[...]
    update = None
    for n in range(0, hidden, 256):
        pre = mxu(normed, expand[:, n : n + 256], 1, 0)
        act, slope = gelu_parts(pre)
        act = act.astype(BF16)
        slope_out[:, n : n + 256] = slope.astype(BF16)
        term = mxu(act, reduce[n : n + 256], 1, 0)
        update = term if update is None else update + term
        reduce_sum[:, n : n + 256] += mxu(cot, act, 0, 0)
    factor = live_factor(slot_ref, s)
    for grp in range(groups):
        lanes = slice(grp * LANES, (grp + 1) * LANES)
        first = pl.multiple_of(s * area, 8)
        total = cells[grp, pl.ds(first, area)] + update[:, lanes]
        out[:, lanes] = (total * factor).astype(BF16)

    @pl.when(s == slots - 1)
    def _():
        reduce_out[...] = jnp.transpose(reduce_sum[...]).astype(BF16)


def backward_body(
    slot_ref,
    side_sends,
    corner_sends,
    cotangent,
    unit_ref,
    scale_ref,
    slope_ref,
    expand,
    reduce,
    grad_out,
    expand_out,
    send,
    expand_sum,
    cells,
    side,
    corner,
    *,
    edge,
):
    s = pl.program_id(0)
    slots = pl.num_programs(0)
    groups = cells.shape[0]
    area = edge * edge
    hidden = expand.shape[1]

    @pl.when(s == 0)
    def _():
        expand_sum[...] = jnp.zeros_like(expand_sum)

    factor = live_factor(slot_ref, s)
    cot = (cotangent[...].astype(F32) * factor).astype(BF16)
    unit = unit_ref[...]
    normed = unit.astype(BF16)
    grad_norm = None
    for n in range(0, hidden, 256):
        grad_act = mxu(cot, reduce[n : n + 256], 1, 1)
        grad_pre = (grad_act * slope_ref[:, n : n + 256].astype(F32)).astype(BF16)
        expand_sum[:, n : n + 256] += mxu(normed, grad_pre, 0, 0)
        term = mxu(grad_pre, expand[:, n : n + 256], 1, 1)
        grad_norm = term if grad_norm is None else grad_norm + term
    channels = groups * LANES
    mean = jnp.sum(grad_norm, axis=1, keepdims=True) * (1.0 / channels)
    along = jnp.sum(grad_norm * unit, axis=1, keepdims=True) * (1.0 / channels)
    grad = (scale_ref[...] * (grad_norm - mean - unit * along)).astype(BF16)
    grad_out[...] = grad
    for grp in range(groups):
        first = pl.multiple_of(s * area, 8)
        cells[grp, pl.ds(first, area)] = grad[:, grp * LANES : (grp + 1) * LANES].astype(F32)

    @pl.when(s == slots - 1)
    def _():
        expand_out[...] = expand_sum[...].astype(BF16)
        n_slots = cells.shape[1] // area
        own = 4 * n_slots
        side[own] = jnp.zeros(side.shape[1:], F32)
        corner[...] = jnp.zeros_like(corner)
        own_records(cells, side, corner, 0, edge, n_slots)
        send_records(send, side, corner, side_sends, corner_sends, own)


def middle_body(padded_field, grad_ref, kernel_ref, spread, kernel_out, padded, taps, sums, *, edge):
    s = pl.program_id(0)
    groups = padded.shape[0]

    @pl.when(s == 0)
    def _():
        padded[...] = jnp.zeros_like(padded)
        spread_taps(taps, kernel_ref)
        sums[...] = jnp.zeros_like(sums)

    for grp in range(groups):
        for i in range(edge):
            row = grad_ref[i * edge : (i + 1) * edge, grp * LANES : (grp + 1) * LANES]
            padded[grp, RIM + i, COL0 : COL0 + edge] = row.astype(F32)

    def one_group(grp, carry):
        kernel_grad_group(padded_field, padded, sums, grp, edge)

        def emit(blk, row, total):
            spread[0, grp, row, 8 * blk : 8 * blk + 8] = total

        conv_group(padded, taps, grp, edge, "own", True, emit)
        return carry

    lax.fori_loop(0, groups, one_group, 0)

    @pl.when(s == pl.num_programs(0) - 1)
    def _():
        for grp in range(groups):
            lanes = slice(grp * LANES, (grp + 1) * LANES)
            kernel_out[:, lanes] = jnp.sum(sums[grp], axis=1)


def final_body(
    slot_ref,
    side_sources,
    corner_sources,
    recv,
    grad_ref,
    spread_own,
    cotangent,
    kernel_ref,
    out,
    side,
    corner,
    cells,
    padded,
    taps,
    *,
    edge,
    cap,
):
    s = pl.program_id(0)
    groups = taps.shape[0]
    area = edge * edge
    n_slots = grad_ref.shape[0] // area
    base = recv.shape[0] * cap
    zero_at = base + 4 * n_slots

    @pl.when(s == 0)
    def _():
        for grp in range(groups):
            cells[grp] = grad_ref[:, grp * LANES : (grp + 1) * LANES].astype(F32)
        side[zero_at] = jnp.zeros(side.shape[1:], F32)
        corner[zero_at] = jnp.zeros(corner.shape[1:], F32)
        received_records(recv, side, corner, cap)
        own_records(cells, side, corner, base, edge, n_slots)
        spread_taps(taps, kernel_ref)
        padded[...] = jnp.zeros_like(padded)

    place_rim(padded, side, corner, side_sources, corner_sources, s, zero_at, edge)
    factor = live_factor(slot_ref, s)
    for grp in range(groups):

        def emit(blk, row, total):
            cells_at = slice(8 * blk, 8 * blk + 8)
            own = spread_own[0, grp, row, cells_at]
            both = own if total is None else own + total
            lanes = slice(grp * LANES, (grp + 1) * LANES)
            first = row * edge + 8 * blk
            cot = cotangent[first : first + 8, lanes].astype(F32)
            out[first : first + 8, lanes] = ((cot + both) * factor).astype(BF16)

        conv_group(padded, taps, grp, edge, "rim", True, emit)


def call(body, name, grid, ins, outs, scratch, flops=0, moved=0, prefetch=0):
    in_specs = []
    for array, block, index in ins:
        if block is None:
            in_specs.append(pl.BlockSpec(memory_space=pltpu.SMEM))
        else:
            in_specs.append(pl.BlockSpec(block, index))
    return pl.pallas_call(
        body,
        name=name,
        grid=grid,
        in_specs=in_specs,
        out_specs=[pl.BlockSpec(block, index) for _, _, block, index in outs],
        out_shape=[jax.ShapeDtypeStruct(shape, dtype) for shape, dtype, _, _ in outs],
        scratch_shapes=scratch,
        compiler_params=pltpu.CompilerParams(vmem_limit_bytes=VMEM_LIMIT),
        cost_estimate=pl.CostEstimate(flops=flops, bytes_accessed=moved, transcendentals=0),
    )(*[array for array, _, _ in ins])


def whole(array):
    rank = array.ndim
    return (array, array.shape, lambda s: (0,) * rank)


def swap(blocks, axis):
    return lax.all_to_all(blocks, axis, split_axis=0, concat_axis=0, tiled=True)


def sum_everywhere(part, basins, tiles):
    rows, columns = part.shape
    blocks = swap(part.reshape(basins, rows // basins, columns), "basin")
    mine = jnp.sum(blocks.astype(F32), axis=0).astype(BF16)
    blocks = swap(mine.reshape(tiles, rows // basins // tiles, columns), "tile")
    mine = jnp.sum(blocks.astype(F32), axis=0).astype(BF16)
    blocks = swap(jnp.broadcast_to(mine[None], (tiles,) + mine.shape), "tile")
    mine = blocks.reshape(rows // basins, columns)
    blocks = swap(jnp.broadcast_to(mine[None], (basins,) + mine.shape), "basin")
    return blocks.reshape(rows, columns)


def sum_small(part, basins, tiles):
    for axis, size in (("basin", basins), ("tile", tiles)):
        blocks = swap(jnp.broadcast_to(part[None], (size,) + part.shape), axis)
        part = jnp.sum(blocks, axis=0)
    return part


def on_device(
    ocean_fields,
    slot_tiles,
    side_sources,
    corner_sources,
    side_sends,
    corner_sends,
    depth_kernel,
    expand_weight,
    reduce_weight,
    field_cotangent,
):
    slots, edge, _, channels = ocean_fields.shape
    hidden = expand_weight.shape[1]
    tiles = lax.axis_size("tile")
    basins = lax.axis_size("basin")
    cap = side_sends.shape[2]
    groups = channels // LANES
    area = edge * edge
    cells = slots * area
    n_side = RIM * edge
    n_corner = 16
    send_rows = cap * (n_side + n_corner)
    table = tiles * cap + 4 * slots + 1
    wide = edge + 2 * COL0
    tall = edge + 2 * RIM

    side_sends = side_sends.reshape(-1)
    corner_sends = corner_sends.reshape(-1)
    side_sources = side_sources.reshape(-1)
    corner_sources = corner_sources.reshape(-1)
    cot_rows = field_cotangent.reshape(cells, channels)
    scalar = lambda array: (array, None, None)
    by_slot = lambda array, width: (array, (area, width), lambda s: (s, 0))
    taps = pltpu.VMEM((groups, TAPS, 8, LANES), F32)
    cell_scratch = pltpu.VMEM((groups, cells, LANES), F32)
    padded_scratch = pltpu.VMEM((groups, tall, wide, LANES), F32)
    own_side = pltpu.VMEM((4 * slots + 1, groups, n_side, LANES), F32)
    own_corner = pltpu.VMEM((4 * slots + 1, groups, n_corner, LANES), F32)
    all_side = pltpu.VMEM((table, groups, n_side, LANES), F32)
    all_corner = pltpu.VMEM((table, groups, n_corner, LANES), F32)
    send_out = ((tiles, send_rows, channels), BF16, (tiles, send_rows, channels), lambda s: (0, 0, 0))
    tile_block = (1, groups, edge, edge, LANES)
    tile_out = ((slots,) + tile_block[1:], F32, tile_block, lambda s: (s, 0, 0, 0, 0))
    mlp_flops = 6 * cells * channels * hidden
    field_bytes = cells * channels * 4

    (send,) = call(
        functools.partial(pack_body, edge=edge),
        "pack_field",
        (1,),
        [scalar(slot_tiles), scalar(side_sends), scalar(corner_sends), whole(ocean_fields)],
        [send_out],
        [cell_scratch, own_side, own_corner],
        moved=field_bytes,
    )
    recv = swap(send, "tile")
    (mixed_own,) = call(
        functools.partial(own_body, edge=edge),
        "mix_own",
        (slots,),
        [
            scalar(slot_tiles),
            (ocean_fields, (1, edge, edge, channels), lambda s: (s, 0, 0, 0)),
            whole(depth_kernel),
        ],
        [tile_out],
        [padded_scratch, taps],
        flops=mlp_flops,
        moved=2 * field_bytes,
    )
    next_rows, padded, unit, scale, slope, reduce_part = call(
        functools.partial(forward_body, edge=edge, cap=cap),
        "forward",
        (slots,),
        [
            scalar(slot_tiles),
            scalar(side_sources),
            scalar(corner_sources),
            whole(recv),
            whole(ocean_fields),
            (mixed_own, tile_block, lambda s: (s, 0, 0, 0, 0)),
            by_slot(cot_rows, channels),
            whole(depth_kernel),
            whole(expand_weight),
            whole(reduce_weight),
        ],
        [
            ((cells, channels), BF16, (area, channels), lambda s: (s, 0)),
            (
                (slots, groups, tall, wide, LANES),
                F32,
                (1, groups, tall, wide, LANES),
                lambda s: (s, 0, 0, 0, 0),
            ),
            ((cells, channels), F32, (area, channels), lambda s: (s, 0)),
            ((cells, 1), F32, (area, 1), lambda s: (s, 0)),
            ((cells, hidden), BF16, (area, hidden), lambda s: (s, 0)),
            ((hidden, channels), BF16, (hidden, channels), lambda s: (0, 0)),
        ],
        [
            all_side,
            all_corner,
            cell_scratch,
            taps,
            pltpu.VMEM((groups, area, LANES), F32),
            pltpu.VMEM((channels, hidden), F32),
        ],
        flops=mlp_flops,
        moved=6 * field_bytes,
    )
    reduce_total = sum_everywhere(reduce_part, basins, tiles)
    grad_rows, expand_part, send = call(
        functools.partial(backward_body, edge=edge),
        "backward",
        (slots,),
        [
            scalar(slot_tiles),
            scalar(side_sends),
            scalar(corner_sends),
            by_slot(cot_rows, channels),
            by_slot(unit, channels),
            (scale, (area, 1), lambda s: (s, 0)),
            by_slot(slope, hidden),
            whole(expand_weight),
            whole(reduce_weight),
        ],
        [
            ((cells, channels), BF16, (area, channels), lambda s: (s, 0)),
            ((channels, hidden), BF16, (channels, hidden), lambda s: (0, 0)),
            send_out,
        ],
        [pltpu.VMEM((channels, hidden), F32), cell_scratch, own_side, own_corner],
        flops=mlp_flops,
        moved=5 * field_bytes,
    )
    recv = swap(send, "tile")
    expand_total = sum_everywhere(expand_part, basins, tiles)
    spread_own, kernel_part = call(
        functools.partial(middle_body, edge=edge),
        "middle",
        (slots,),
        [
            (padded, (1, groups, tall, wide, LANES), lambda s: (s, 0, 0, 0, 0)),
            by_slot(grad_rows, channels),
            whole(depth_kernel),
        ],
        [tile_out, ((TAPS, channels), F32, (TAPS, channels), lambda s: (0, 0))],
        [padded_scratch, taps, taps],
        flops=2 * mlp_flops,
        moved=4 * field_bytes,
    )
    kernel_total = sum_small(kernel_part, basins, tiles)
    (grad_field,) = call(
        functools.partial(final_body, edge=edge, cap=cap),
        "final",
        (slots,),
        [
            scalar(slot_tiles),
            scalar(side_sources),
            scalar(corner_sources),
            whole(recv),
            whole(grad_rows),
            (spread_own, tile_block, lambda s: (s, 0, 0, 0, 0)),
            by_slot(cot_rows, channels),
            whole(depth_kernel),
        ],
        [((cells, channels), BF16, (area, channels), lambda s: (s, 0))],
        [all_side, all_corner, cell_scratch, padded_scratch, taps],
        flops=mlp_flops // 2,
        moved=3 * field_bytes,
    )
    factor = 1.0 / math.sqrt(basins * tiles * cells)
    shape = ocean_fields.shape
    return (
        next_rows.reshape(shape),
        grad_field.reshape(shape),
        kernel_total * factor,
        expand_total.astype(F32) * factor,
        reduce_total.astype(F32) * factor,
    )


def solution(mesh):
    split = ("basin", "tile")
    field = P(split, None, None, None)
    table = P(split, None, None)
    pair = P(split, None)
    return jax.shard_map(
        on_device,
        mesh=mesh,
        in_specs=(field, P(split), pair, pair, table, table, P(), P(), P(), field),
        out_specs=(field, field, P(), P(), P()),
        check_vma=False,
    )
```

```python
import functools
import math

import jax
import jax.numpy as jnp
from jax import lax
from jax.experimental import pallas as pl
from jax.experimental.pallas import tpu as pltpu
from jax.sharding import PartitionSpec as P


KERNEL = 7
TAPS = KERNEL * KERNEL
RIM = 3
LANES = 128
COL0 = 8
LN_EPS = 1e-06
F32 = jnp.float32
BF16 = jnp.bfloat16
VMEM_LIMIT = 60 * 1024 * 1024


def mxu(lhs, rhs, lhs_dim, rhs_dim):
    return lax.dot_general(
        lhs, rhs, (((lhs_dim,), (rhs_dim,)), ((), ())), preferred_element_type=F32
    )


def gelu_parts(pre):
    cdf = 0.5 * (1.0 + lax.erf(pre * (1.0 / math.sqrt(2.0))))
    density = jnp.exp(-0.5 * pre * pre) * (1.0 / math.sqrt(2.0 * math.pi))
    return pre * cdf, cdf + pre * density


def live_factor(slot_ref, slot):
    return jnp.where(slot_ref[slot] >= 0, 1.0, 0.0).astype(F32)


def own_records(cells, side, corner, base, edge, slots):
    area = edge * edge
    rim_rows = RIM * edge
    far = edge - RIM
    for grp in range(cells.shape[0]):
        for s in range(slots):
            at = base + 4 * s
            start = s * area
            side[at, grp] = cells[grp, start : start + rim_rows]
            side[at + 1, grp] = cells[grp, start + area - rim_rows : start + area]
            for c in range(RIM):
                rows = slice(c * edge, (c + 1) * edge)
                side[at + 2, grp, rows] = cells[grp, pl.ds(start + c, edge, stride=edge)]
                side[at + 3, grp, rows] = cells[grp, pl.ds(start + far + c, edge, stride=edge)]
            for e in range(4):
                row0 = far if e // 2 else 0
                col0 = far if e % 2 else 0
                for r in range(RIM):
                    first = start + (row0 + r) * edge + col0
                    corner[at + e, grp, RIM * r : RIM * r + RIM] = cells[grp, first : first + RIM]


def send_records(send, side, corner, side_sends, corner_sends, zero_at, base=0):
    peers = send.shape[0]
    groups = side.shape[1]
    cap = side_sends.shape[2]

    def one_peer(p, carry):
        for grp in range(groups):
            pieces = []
            for table, sends in ((side, side_sends), (corner, corner_sends)):
                for k in range(cap):
                    code = sends[0, p, k]
                    pieces.append(table[jnp.where(code < 0, zero_at, code + base), grp])
            block = jnp.concatenate(pieces, axis=0)
            send[p, :, grp * LANES : (grp + 1) * LANES] = block.astype(BF16)
        return carry

    lax.fori_loop(0, peers, one_peer, 0)


def received_records(recv, side, corner, cap):
    groups = side.shape[1]
    n_side = side.shape[2]
    n_corner = corner.shape[2]

    def one_peer(p, carry):
        for grp in range(groups):
            block = recv[p, :, grp * LANES : (grp + 1) * LANES].astype(F32)
            for k in range(cap):
                side[p * cap + k, grp] = block[k * n_side : (k + 1) * n_side]
                first = cap * n_side + k * n_corner
                corner[p * cap + k, grp] = block[first : first + n_corner]
        return carry

    lax.fori_loop(0, recv.shape[0], one_peer, 0)


def place_rim(padded, side, corner, side_sources, corner_sources, slot, zero_at, edge):
    for e in range(4):
        code = side_sources[slot, e]
        at = jnp.where(code < 0, zero_at, code)
        for grp in range(side.shape[1]):
            for c in range(RIM):
                piece = side[at, grp, c * edge : (c + 1) * edge]
                if e < 2:
                    row = c if e == 0 else RIM + edge + c
                    padded[grp, row, COL0 : COL0 + edge] = piece
                else:
                    col = COL0 - RIM + c if e == 2 else COL0 + edge + c
                    padded[grp, RIM : RIM + edge, col] = piece
        code = corner_sources[slot, e]
        at = jnp.where(code < 0, zero_at, code)
        row0 = RIM + edge if e // 2 else 0
        col0 = COL0 + edge if e % 2 else COL0 - RIM
        for grp in range(side.shape[1]):
            for r in range(RIM):
                padded[grp, row0 + r, col0 : col0 + RIM] = corner[
                    at, grp, RIM * r : RIM * r + RIM
                ]


def spread_taps(taps, kernel_ref):
    for grp in range(taps.shape[0]):
        for t in range(TAPS):
            row = kernel_ref[t : t + 1, grp * LANES : (grp + 1) * LANES].astype(F32)
            taps[grp, t] = jnp.broadcast_to(row, taps.shape[2:])


def conv_group(padded, taps, grp, edge, part, flipped, emit):
    blocks = edge // 8
    lane = lax.broadcasted_iota(jnp.int32, (8, LANES), 0)
    for blk in range(blocks):
        acc = [None] * edge
        for b in range(KERNEL):
            west = part == "rim" and blk == 0 and b < RIM
            east = part == "rim" and blk == blocks - 1 and b > RIM
            weights = []
            for a in range(KERNEL):
                t = a * KERNEL + b
                weights.append(taps[grp, TAPS - 1 - t if flipped else t])
            for r in range(edge + 2 * RIM):
                inner = RIM <= r < RIM + edge
                if part == "own" and not inner:
                    continue
                if part == "rim" and inner and not (west or east):
                    continue
                first = COL0 - RIM + b + 8 * blk
                cells = padded[grp, r, first : first + 8]
                if part == "rim" and inner:
                    keep = lane < RIM - b if west else lane >= 8 + RIM - b
                    cells = jnp.where(keep, cells, 0.0)
                for a in range(KERNEL):
                    row = r - a
                    if 0 <= row < edge:
                        term = cells * weights[a]
                        acc[row] = term if acc[row] is None else acc[row] + term
        for row in range(edge):
            emit(blk, row, acc[row])


def kernel_grad_group(padded, grad, sums, grp, edge):
    for b in range(KERNEL):
        acc = [None] * KERNEL
        for blk in range(edge // 8):
            rows = [grad[grp, RIM + i, COL0 + 8 * blk : COL0 + 8 * blk + 8] for i in range(edge)]
            for r in range(edge + 2 * RIM):
                first = COL0 - RIM + b + 8 * blk
                cells = padded[0, grp, r, first : first + 8]
                for a in range(KERNEL):
                    if 0 <= r - a < edge:
                        term = rows[r - a] * cells
                        acc[a] = term if acc[a] is None else acc[a] + term
        for a in range(KERNEL):
            sums[grp, a * KERNEL + b] += acc[a]


def pack_body(slot_ref, side_sends, corner_sends, field, send, cells, side, corner, *, edge):
    slots = field.shape[0]
    own = 4 * slots
    area = edge * edge
    for s in range(slots):
        factor = live_factor(slot_ref, s)
        for grp in range(cells.shape[0]):
            for i in list(range(edge)):
                row = field[s, i, :, grp * LANES : (grp + 1) * LANES].astype(F32)
                first = s * area + i * edge
                cells[grp, first : first + edge] = row * factor
    side[own] = jnp.zeros(side.shape[1:], F32)
    corner[...] = jnp.zeros_like(corner)
    own_records(cells, side, corner, 0, edge, slots)
    send_records(send, side, corner, side_sends, corner_sends, own)


def own_body(slot_ref, field, kernel_ref, mixed, padded, taps, *, edge):
    s = pl.program_id(0)
    groups = padded.shape[0]

    @pl.when(s == 0)
    def _():
        padded[...] = jnp.zeros_like(padded)
        spread_taps(taps, kernel_ref)

    factor = live_factor(slot_ref, s)
    for grp in range(groups):
        for i in range(edge):
            row = field[0, i, :, grp * LANES : (grp + 1) * LANES].astype(F32)
            padded[grp, RIM + i, COL0 : COL0 + edge] = row * factor

    def one_group(grp, carry):
        def emit(blk, row, total):
            mixed[0, grp, row, 8 * blk : 8 * blk + 8] = total

        conv_group(padded, taps, grp, edge, "own", False, emit)
        return carry

    lax.fori_loop(0, groups, one_group, 0)


def mlp_body(
    slot_ref,
    side_sources,
    corner_sources,
    side_sends,
    corner_sends,
    recv,
    field,
    mixed_own,
    cotangent,
    kernel_ref,
    expand,
    reduce,
    out,
    padded_out,
    grad_out,
    weights_out,
    send,
    side,
    corner,
    cells,
    taps,
    mixed,
    unit_ref,
    reduce_sum,
    expand_sum,
    *,
    edge,
    cap,
):
    s = pl.program_id(0)
    slots = pl.num_programs(0)
    groups = taps.shape[0]
    area = edge * edge
    n_slots = field.shape[0]
    base = recv.shape[0] * cap
    zero_at = base + 4 * n_slots
    hidden = expand.shape[1]
    channels = groups * LANES

    @pl.when(s == 0)
    def _():
        for t in range(n_slots):
            factor = live_factor(slot_ref, t)
            for grp in range(groups):
                for i in range(edge):
                    row = field[t, i, :, grp * LANES : (grp + 1) * LANES].astype(F32)
                    first = t * area + i * edge
                    cells[grp, first : first + edge] = row * factor
        side[zero_at] = jnp.zeros(side.shape[1:], F32)
        corner[...] = jnp.zeros_like(corner)
        received_records(recv, side, corner, cap)
        own_records(cells, side, corner, base, edge, n_slots)
        spread_taps(taps, kernel_ref)
        reduce_sum[...] = jnp.zeros_like(reduce_sum)
        expand_sum[...] = jnp.zeros_like(expand_sum)

    padded = padded_out.at[0]
    for grp in range(groups):
        for i in range(edge):
            first = pl.multiple_of(s * area + i * edge, 8)
            padded[grp, RIM + i, COL0 : COL0 + edge] = cells[grp, pl.ds(first, edge)]
    place_rim(padded, side, corner, side_sources, corner_sources, s, zero_at, edge)

    def one_group(grp, carry):
        def emit(blk, row, total):
            own = mixed_own[0, grp, row, 8 * blk : 8 * blk + 8]
            first = row * edge + 8 * blk
            mixed[grp, first : first + 8] = own if total is None else own + total

        conv_group(padded, taps, grp, edge, "rim", False, emit)
        return carry

    lax.fori_loop(0, groups, one_group, 0)

    factor = live_factor(slot_ref, s)
    parts = [mixed[grp] for grp in range(groups)]
    mean = sum(jnp.sum(part, axis=1, keepdims=True) for part in parts) * (1.0 / channels)
    parts = [part - mean for part in parts]
    var = sum(jnp.sum(part * part, axis=1, keepdims=True) for part in parts) * (1.0 / channels)
    scale = lax.rsqrt(var + LN_EPS)
    unit = jnp.concatenate([part * scale for part in parts], axis=1)
    unit_ref[...] = unit
    normed = unit.astype(BF16)
    cot = (cotangent[...].astype(F32) * factor).astype(BF16)
    update = None
    grad_norm = None
    for n in range(0, hidden, 256):
        pre = mxu(normed, expand[:, n : n + 256], 1, 0)
        act, slope = gelu_parts(pre)
        act = act.astype(BF16)
        grad_act = mxu(cot, reduce[n : n + 256], 1, 1)
        grad_pre = (grad_act * slope).astype(BF16)
        term = mxu(act, reduce[n : n + 256], 1, 0)
        update = term if update is None else update + term
        reduce_sum[:, n : n + 256] += mxu(cot, act, 0, 0)
        expand_sum[n // 256] += mxu(normed, grad_pre, 0, 0)
        term = mxu(grad_pre, expand[:, n : n + 256], 1, 1)
        grad_norm = term if grad_norm is None else grad_norm + term
    at = pl.ds(pl.multiple_of(s * area, 8), area)
    for grp in range(groups):
        lanes = slice(grp * LANES, (grp + 1) * LANES)
        out[:, lanes] = ((cells[grp, at] + update[:, lanes]) * factor).astype(BF16)

    unit = unit_ref[...]
    mean = jnp.sum(grad_norm, axis=1, keepdims=True) * (1.0 / channels)
    along = jnp.sum(grad_norm * unit, axis=1, keepdims=True) * (1.0 / channels)
    grad = (scale * (grad_norm - mean - unit * along)).astype(BF16)
    grad_out[...] = grad
    for grp in range(groups):
        cells[grp, at] = grad[:, grp * LANES : (grp + 1) * LANES].astype(F32)

    @pl.when(s == slots - 1)
    def _():
        weights_out[:hidden] = jnp.transpose(reduce_sum[...]).astype(BF16)
        for n in range(hidden // 256):
            first = hidden + n * channels
            weights_out[first : first + channels] = expand_sum[n].astype(BF16)
        own_records(cells, side, corner, base, edge, n_slots)
        send_records(send, side, corner, side_sends, corner_sends, zero_at, base)


def fill_padded(padded, grad_ref, edge):
    for grp in range(padded.shape[0]):
        for i in range(edge):
            row = grad_ref[i * edge : (i + 1) * edge, grp * LANES : (grp + 1) * LANES]
            padded[grp, RIM + i, COL0 : COL0 + edge] = row.astype(F32)


def kernel_grad_body(padded_field, grad_ref, kernel_out, padded, sums, *, edge):
    s = pl.program_id(0)
    groups = padded.shape[0]

    @pl.when(s == 0)
    def _():
        sums[...] = jnp.zeros_like(sums)

    fill_padded(padded, grad_ref, edge)

    def one_group(grp, carry):
        kernel_grad_group(padded_field, padded, sums, grp, edge)
        return carry

    lax.fori_loop(0, groups, one_group, 0)

    @pl.when(s == pl.num_programs(0) - 1)
    def _():
        kernel_out[...] = jnp.zeros_like(kernel_out)
        for grp in range(groups):
            lanes = slice(grp * LANES, (grp + 1) * LANES)
            kernel_out[:TAPS, lanes] = jnp.sum(sums[grp], axis=1)


def final_body(
    slot_ref,
    side_sources,
    corner_sources,
    recv,
    grad_ref,
    cotangent,
    kernel_ref,
    *rest,
    edge,
    cap,
    first_slot,
):
    out, cells_out, side, corner, cells, padded, taps = rest[-7:]
    step = pl.program_id(0)
    s = step + first_slot
    groups = taps.shape[0]
    area = edge * edge
    n_slots = grad_ref.shape[0] // area
    base = recv.shape[0] * cap
    zero_at = base + 4 * n_slots

    @pl.when(step == 0)
    def _():
        for grp in range(groups):
            cells[grp] = grad_ref[:, grp * LANES : (grp + 1) * LANES].astype(F32)
        side[zero_at] = jnp.zeros(side.shape[1:], F32)
        corner[zero_at] = jnp.zeros(corner.shape[1:], F32)
        received_records(recv, side, corner, cap)
        own_records(cells, side, corner, base, edge, n_slots)
        spread_taps(taps, kernel_ref)

    for grp in range(groups):
        for i in range(edge):
            first = pl.multiple_of(s * area + i * edge, 8)
            padded[grp, RIM + i, COL0 : COL0 + edge] = cells[grp, pl.ds(first, edge)]
    place_rim(padded, side, corner, side_sources, corner_sources, s, zero_at, edge)
    factor = live_factor(slot_ref, s)

    def one_group(grp, carry):
        def emit(blk, row, total):
            first = row * edge + 8 * blk
            cells_out[grp, first : first + 8] = total

        conv_group(padded, taps, grp, edge, "all", True, emit)
        return carry

    lax.fori_loop(0, groups, one_group, 0)
    for grp in range(groups):
        lanes = slice(grp * LANES, (grp + 1) * LANES)
        total = cotangent[:, lanes].astype(F32) + cells_out[grp]
        out[:, lanes] = (total * factor).astype(BF16)


def weights_body(order, *refs, hidden, factor):
    blocks, (kernel_out, expand_out, reduce_out, rows) = refs[:-4], refs[-4:]
    channels = reduce_out.shape[1]
    part = 2 * hidden // len(blocks)
    kernel_sum = None
    for at, block in enumerate(blocks):
        first = pl.multiple_of(order[at] * part, 8)
        rows[pl.ds(first, part)] = block[:part].astype(F32) * factor
        kernel = block[part:].astype(F32)
        kernel_sum = kernel if kernel_sum is None else kernel_sum + kernel
    kernel_out[...] = kernel_sum[:TAPS] * factor
    reduce_out[...] = rows[:hidden]
    for n in range(hidden // 256):
        first = hidden + n * channels
        expand_out[:, n * 256 : (n + 1) * 256] = rows[first : first + channels]


def call(body, grid, ins, outs, scratch, flops=0, moved=0, aliases=None):
    in_specs = []
    for array, block, index in ins:
        if block is None:
            in_specs.append(pl.BlockSpec(memory_space=index or pltpu.SMEM))
        else:
            in_specs.append(pl.BlockSpec(block, index))
    return pl.pallas_call(
        body,
        grid=grid,
        in_specs=in_specs,
        out_specs=[pl.BlockSpec(block, index) for _, _, block, index in outs],
        out_shape=[jax.ShapeDtypeStruct(shape, dtype) for shape, dtype, _, _ in outs],
        scratch_shapes=scratch,
        input_output_aliases=aliases or {},
        compiler_params=pltpu.CompilerParams(vmem_limit_bytes=VMEM_LIMIT),
        cost_estimate=pl.CostEstimate(flops=flops, bytes_accessed=moved, transcendentals=0),
    )(*[array for array, _, _ in ins])


def whole(array):
    rank = array.ndim
    return (array, array.shape, lambda s: (0,) * rank)


def swap(blocks, axis):
    return lax.all_to_all(blocks, axis, split_axis=0, concat_axis=0, tiled=True)


def spread_blocks(blocks, axis):
    size = blocks.shape[0]
    me = lax.axis_index(axis)
    take = lambda at: lax.dynamic_index_in_dim(blocks, at, 0, keepdims=False)
    parts = [take(me)]
    for step in range(1, size):
        perm = [(i, (i + step) % size) for i in range(size)]
        parts.append(lax.ppermute(take((me + step) % size), axis, perm))
    return parts


def gather_blocks(block, axis):
    size = lax.axis_size(axis)
    me = lax.axis_index(axis)
    swap_pair = [(i, i ^ 1) for i in range(size)]
    parts = [block]
    order = [me]
    for step in range(2, size, 2):
        perm = [(i, (i + step) % size) for i in range(size)]
        parts.append(lax.ppermute(block, axis, perm))
        order.append((me - step) % size)
    passed = [lax.ppermute(part, axis, swap_pair) for part in parts]
    partner = me ^ 1
    order += [partner] + [(partner - step) % size for step in range(2, size, 2)]
    return parts + passed, jnp.stack(order).astype(jnp.int32)


def on_device(
    ocean_fields,
    slot_tiles,
    side_sources,
    corner_sources,
    side_sends,
    corner_sends,
    depth_kernel,
    expand_weight,
    reduce_weight,
    field_cotangent,
):
    slots, edge, _, channels = ocean_fields.shape
    hidden = expand_weight.shape[1]
    tiles = lax.axis_size("tile")
    basins = lax.axis_size("basin")
    cap = side_sends.shape[2]
    groups = channels // LANES
    area = edge * edge
    cells = slots * area
    n_side = RIM * edge
    n_corner = 16
    send_rows = cap * (n_side + n_corner)
    table = tiles * cap + 4 * slots + 1
    wide = edge + 2 * COL0
    tall = edge + 2 * RIM

    cot_rows = field_cotangent.reshape(cells, channels)
    scalar = lambda array: (array, None, None)
    by_slot = lambda array, width: (array, (area, width), lambda s: (s, 0))
    taps = pltpu.VMEM((groups, TAPS, 8, LANES), F32)
    cell_scratch = pltpu.VMEM((groups, cells, LANES), F32)
    padded_scratch = pltpu.VMEM((groups, tall, wide, LANES), F32)
    own_side = pltpu.VMEM((4 * slots + 1, groups, n_side, LANES), F32)
    own_corner = pltpu.VMEM((4 * slots + 1, groups, n_corner, LANES), F32)
    all_side = pltpu.VMEM((table, groups, n_side, LANES), F32)
    all_corner = pltpu.VMEM((table, groups, n_corner, LANES), F32)
    send_out = ((tiles, send_rows, channels), BF16, (tiles, send_rows, channels), lambda s: (0, 0, 0))
    tile_block = (1, groups, edge, edge, LANES)
    tile_out = ((slots,) + tile_block[1:], F32, tile_block, lambda s: (s, 0, 0, 0, 0))
    kernel_rows = tiles * 8 * -(-TAPS // (8 * tiles))
    mlp_flops = 6 * cells * channels * hidden
    field_bytes = cells * channels * 4

    (send,) = call(
        functools.partial(pack_body, edge=edge),
        (1,),
        [scalar(slot_tiles), scalar(side_sends), scalar(corner_sends), whole(ocean_fields)],
        [send_out],
        [cell_scratch, own_side, own_corner],
        moved=field_bytes,
    )
    recv = swap(send, "tile")
    (mixed_own,) = call(
        functools.partial(own_body, edge=edge),
        (slots,),
        [
            scalar(slot_tiles),
            (ocean_fields, (1, edge, edge, channels), lambda s: (s, 0, 0, 0)),
            whole(depth_kernel),
        ],
        [tile_out],
        [padded_scratch, taps],
        flops=mlp_flops,
        moved=2 * field_bytes,
    )
    next_rows, padded, grad_rows, weights, send = call(
        functools.partial(mlp_body, edge=edge, cap=cap),
        (slots,),
        [
            scalar(slot_tiles),
            scalar(side_sources),
            scalar(corner_sources),
            scalar(side_sends),
            scalar(corner_sends),
            whole(recv),
            whole(ocean_fields),
            (mixed_own, tile_block, lambda s: (s, 0, 0, 0, 0)),
            by_slot(cot_rows, channels),
            whole(depth_kernel),
            whole(expand_weight),
            whole(reduce_weight),
        ],
        [
            ((cells, channels), BF16, (area, channels), lambda s: (s, 0)),
            (
                (slots, groups, tall, wide, LANES),
                F32,
                (1, groups, tall, wide, LANES),
                lambda s: (s, 0, 0, 0, 0),
            ),
            ((cells, channels), BF16, (area, channels), lambda s: (s, 0)),
            ((2 * hidden, channels), BF16, (2 * hidden, channels), lambda s: (0, 0)),
            send_out,
        ],
        [
            all_side,
            all_corner,
            cell_scratch,
            taps,
            pltpu.VMEM((groups, area, LANES), F32),
            pltpu.VMEM((area, channels), F32),
            pltpu.VMEM((channels, hidden), F32),
            pltpu.VMEM((hidden // 256, channels, 256), F32),
        ],
        flops=2 * mlp_flops,
        moved=6 * field_bytes,
    )
    recv = swap(send, "tile")
    rows = 2 * hidden
    blocks = spread_blocks(weights.reshape(basins, rows // basins, channels), "basin")
    (kernel_part,) = call(
        functools.partial(kernel_grad_body, edge=edge),
        (slots,),
        [
            (padded, (1, groups, tall, wide, LANES), lambda s: (s, 0, 0, 0, 0)),
            by_slot(grad_rows, channels),
        ],
        [((kernel_rows, channels), F32, (kernel_rows, channels), lambda s: (0, 0))],
        [padded_scratch, taps],
        flops=mlp_flops,
        moved=4 * field_bytes,
    )
    mine = sum(block.astype(F32) for block in blocks).astype(BF16)
    part = rows // basins // tiles
    mine = jnp.concatenate(
        [
            mine.reshape(tiles, part, channels),
            kernel_part.astype(BF16).reshape(tiles, kernel_rows // tiles, channels),
        ],
        axis=1,
    )
    blocks = swap(mine, "tile")
    half = slots // 2

    def final(first_slot, count, previous):
        rows_at = lambda s: (s + first_slot, 0)
        ins = [
            scalar(slot_tiles),
            scalar(side_sources),
            scalar(corner_sources),
            whole(recv),
            whole(grad_rows),
            (cot_rows, (area, channels), rows_at),
            whole(depth_kernel),
        ]
        if previous is not None:
            ins.append((previous, None, pl.ANY))
        (rows_out,) = call(
            functools.partial(final_body, edge=edge, cap=cap, first_slot=first_slot),
            (count,),
            ins,
            [((cells, channels), BF16, (area, channels), rows_at)],
            [
                pltpu.VMEM((groups, area, LANES), F32),
                all_side,
                all_corner,
                cell_scratch,
                padded_scratch,
                taps,
            ],
            flops=mlp_flops // 2,
            moved=3 * field_bytes,
            aliases=None if previous is None else {len(ins) - 1: 0},
        )
        return rows_out

    grad_field = final(0, half, None)
    mine = jnp.sum(blocks.astype(F32), axis=0).astype(BF16)
    blocks = swap(jnp.broadcast_to(mine[None], (tiles,) + mine.shape), "tile")
    mine = jnp.concatenate(
        [
            blocks[:, :part].reshape(rows // basins, channels),
            blocks[:, part:].reshape(kernel_rows, channels),
        ],
        axis=0,
    )
    blocks, order = gather_blocks(mine, "basin")
    grad_field = final(half, slots - half, grad_field)
    factor = 1.0 / math.sqrt(basins * tiles * cells)
    kernel_total, expand_total, reduce_total = call(
        functools.partial(weights_body, hidden=hidden, factor=factor),
        (1,),
        [scalar(order)] + [whole(block) for block in blocks],
        [
            ((TAPS, channels), F32, (TAPS, channels), lambda s: (0, 0)),
            ((channels, hidden), F32, (channels, hidden), lambda s: (0, 0)),
            ((hidden, channels), F32, (hidden, channels), lambda s: (0, 0)),
        ],
        [pltpu.VMEM((rows, channels), F32)],
        moved=6 * hidden * channels * 2,
    )
    shape = ocean_fields.shape
    return (
        next_rows.reshape(shape),
        grad_field.reshape(shape),
        kernel_total,
        expand_total,
        reduce_total,
    )


def solution(mesh):
    split = ("basin", "tile")
    field = P(split, None, None, None)
    table = P(split, None, None)
    pair = P(split, None)

    return jax.shard_map(
        on_device,
        mesh=mesh,
        in_specs=(field, P(split), pair, pair, table, table, P(), P(), P(), field),
        out_specs=(field, field, P(), P(), P()),
        check_vma=False,
    )
```

```python
import functools
import math

import jax
import jax.numpy as jnp
from jax import lax
from jax.experimental import pallas as pl
from jax.experimental.pallas import tpu as pltpu
from jax.sharding import PartitionSpec as P


KERNEL = 7
TAPS = KERNEL * KERNEL
RIM = 3
LANES = 128
COL0 = 8
LN_EPS = 1e-06
F32 = jnp.float32
BF16 = jnp.bfloat16
VMEM_LIMIT = 60 * 1024 * 1024


def mxu(lhs, rhs, lhs_dim, rhs_dim):
    return lax.dot_general(
        lhs, rhs, (((lhs_dim,), (rhs_dim,)), ((), ())), preferred_element_type=F32
    )


def gelu_parts(pre):
    cdf = 0.5 * (1.0 + lax.erf(pre * (1.0 / math.sqrt(2.0))))
    density = jnp.exp(-0.5 * pre * pre) * (1.0 / math.sqrt(2.0 * math.pi))
    return pre * cdf, cdf + pre * density


def live_factor(slot_ref, slot):
    return jnp.where(slot_ref[slot] >= 0, 1.0, 0.0).astype(F32)


def own_records(cells, side, corner, base, edge, slots):
    area = edge * edge
    rim_rows = RIM * edge
    far = edge - RIM
    for grp in range(cells.shape[0]):
        for s in range(slots):
            at = base + 4 * s
            start = s * area
            side[at, grp] = cells[grp, start : start + rim_rows]
            side[at + 1, grp] = cells[grp, start + area - rim_rows : start + area]
            for c in range(RIM):
                rows = slice(c * edge, (c + 1) * edge)
                side[at + 2, grp, rows] = cells[grp, pl.ds(start + c, edge, stride=edge)]
                side[at + 3, grp, rows] = cells[grp, pl.ds(start + far + c, edge, stride=edge)]
            for e in range(4):
                row0 = far if e // 2 else 0
                col0 = far if e % 2 else 0
                for r in range(RIM):
                    first = start + (row0 + r) * edge + col0
                    corner[at + e, grp, RIM * r : RIM * r + RIM] = cells[grp, first : first + RIM]


def send_records(send, side, corner, side_sends, corner_sends, zero_at, base=0):
    peers = send.shape[0]
    groups = side.shape[1]
    cap = side_sends.shape[0]

    def one_peer(p, carry):
        for grp in range(groups):
            pieces = []
            for table, sends in ((side, side_sends), (corner, corner_sends)):
                for k in range(cap):
                    code = sends[k, p]
                    pieces.append(table[jnp.where(code < 0, zero_at, code + base), grp])
            block = jnp.concatenate(pieces, axis=0)
            send[p, :, grp * LANES : (grp + 1) * LANES] = block.astype(BF16)
        return carry

    lax.fori_loop(0, peers, one_peer, 0)


def received_records(recv, side, corner, cap):
    groups = side.shape[1]
    n_side = side.shape[2]
    n_corner = corner.shape[2]

    def one_peer(p, carry):
        for grp in range(groups):
            block = recv[p, :, grp * LANES : (grp + 1) * LANES].astype(F32)
            for k in range(cap):
                side[p * cap + k, grp] = block[k * n_side : (k + 1) * n_side]
                first = cap * n_side + k * n_corner
                corner[p * cap + k, grp] = block[first : first + n_corner]
        return carry

    lax.fori_loop(0, recv.shape[0], one_peer, 0)


def place_rim(padded, side, corner, side_sources, corner_sources, slot, zero_at, edge):
    for e in range(4):
        code = side_sources[slot, e]
        at = jnp.where(code < 0, zero_at, code)
        for grp in range(side.shape[1]):
            for c in range(RIM):
                piece = side[at, grp, c * edge : (c + 1) * edge]
                if e < 2:
                    row = c if e == 0 else RIM + edge + c
                    padded[grp, row, COL0 : COL0 + edge] = piece
                else:
                    col = COL0 - RIM + c if e == 2 else COL0 + edge + c
                    padded[grp, RIM : RIM + edge, col] = piece
        code = corner_sources[slot, e]
        at = jnp.where(code < 0, zero_at, code)
        row0 = RIM + edge if e // 2 else 0
        col0 = COL0 + edge if e % 2 else COL0 - RIM
        for grp in range(side.shape[1]):
            for r in range(RIM):
                padded[grp, row0 + r, col0 : col0 + RIM] = corner[
                    at, grp, RIM * r : RIM * r + RIM
                ]


def spread_taps(taps, kernel_ref):
    for grp in range(taps.shape[0]):
        for t in range(TAPS):
            row = kernel_ref[t : t + 1, grp * LANES : (grp + 1) * LANES].astype(F32)
            taps[grp, t] = jnp.broadcast_to(row, taps.shape[2:])


def conv_group(padded, taps, grp, edge, part, flipped, emit):
    blocks = edge // 8
    lane = lax.broadcasted_iota(jnp.int32, (8, LANES), 0)
    for blk in range(blocks):
        acc = [None] * edge
        for b in range(KERNEL):
            west = part == "rim" and blk == 0 and b < RIM
            east = part == "rim" and blk == blocks - 1 and b > RIM
            weights = []
            for a in range(KERNEL):
                t = a * KERNEL + b
                weights.append(taps[grp, TAPS - 1 - t if flipped else t])
            for r in range(edge + 2 * RIM):
                inner = RIM <= r < RIM + edge
                if part == "own" and not inner:
                    continue
                if part == "rim" and inner and not (west or east):
                    continue
                first = COL0 - RIM + b + 8 * blk
                cells = padded[grp, r, first : first + 8]
                if part == "rim" and inner:
                    keep = lane < RIM - b if west else lane >= 8 + RIM - b
                    cells = jnp.where(keep, cells, 0.0)
                for a in range(KERNEL):
                    row = r - a
                    if 0 <= row < edge:
                        term = cells * weights[a]
                        acc[row] = term if acc[row] is None else acc[row] + term
        for row in range(edge):
            emit(blk, row, acc[row])


def kernel_grad_group(padded, grad, sums, grp, edge):
    for b in range(KERNEL):
        acc = [None] * KERNEL
        for blk in range(edge // 8):
            rows = [grad[grp, RIM + i, COL0 + 8 * blk : COL0 + 8 * blk + 8] for i in range(edge)]
            for r in range(edge + 2 * RIM):
                first = COL0 - RIM + b + 8 * blk
                cells = padded[0, grp, r, first : first + 8]
                for a in range(KERNEL):
                    if 0 <= r - a < edge:
                        term = rows[r - a] * cells
                        acc[a] = term if acc[a] is None else acc[a] + term
        for a in range(KERNEL):
            sums[grp, a * KERNEL + b] += acc[a]


def pack_body(slot_ref, side_sends, corner_sends, field, send, cells, side, corner, *, edge):
    slots = field.shape[0]
    own = 4 * slots
    area = edge * edge
    for s in range(slots):
        factor = live_factor(slot_ref, s)
        for grp in range(cells.shape[0]):
            for i in list(range(edge)):
                row = field[s, i, :, grp * LANES : (grp + 1) * LANES].astype(F32)
                first = s * area + i * edge
                cells[grp, first : first + edge] = row * factor
    side[own] = jnp.zeros(side.shape[1:], F32)
    corner[...] = jnp.zeros_like(corner)
    own_records(cells, side, corner, 0, edge, slots)
    send_records(send, side, corner, side_sends, corner_sends, own)


def own_body(
    slot_ref, field, kernel_ref, cotangent, reduce, mixed, grad_act, padded, taps, *, edge
):
    s = pl.program_id(0)
    groups = padded.shape[0]
    share = cotangent.shape[0] // groups

    @pl.when(s == 0)
    def _():
        padded[...] = jnp.zeros_like(padded)
        spread_taps(taps, kernel_ref)

    factor = live_factor(slot_ref, s)
    for grp in range(groups):
        for i in range(edge):
            row = field[0, i, :, grp * LANES : (grp + 1) * LANES].astype(F32)
            padded[grp, RIM + i, COL0 : COL0 + edge] = row * factor

    def one_group(grp, carry):
        def emit(blk, row, total):
            mixed[0, grp, row, 8 * blk : 8 * blk + 8] = total

        rows = pl.ds(pl.multiple_of(grp * share, 16), share)
        cot = (cotangent[rows].astype(F32) * factor).astype(BF16)
        for n in range(0, reduce.shape[0], 256):
            grad_act[rows, n : n + 256] = mxu(cot, reduce[n : n + 256], 1, 1)
        conv_group(padded, taps, grp, edge, "own", False, emit)
        return carry

    lax.fori_loop(0, groups, one_group, 0)


def mlp_body(
    slot_ref,
    side_sources,
    corner_sources,
    side_sends,
    corner_sends,
    recv,
    field,
    mixed_own,
    grad_act_ref,
    cotangent,
    kernel_ref,
    expand,
    reduce,
    out,
    padded_out,
    grad_out,
    weights_out,
    send,
    side,
    corner,
    cells,
    taps,
    mixed,
    unit_ref,
    reduce_sum,
    expand_sum,
    *,
    edge,
    cap,
):
    s = pl.program_id(0)
    slots = pl.num_programs(0)
    groups = taps.shape[0]
    area = edge * edge
    n_slots = field.shape[0]
    base = recv.shape[0] * cap
    zero_at = base + 4 * n_slots
    hidden = expand.shape[1]
    channels = groups * LANES

    @pl.when(s == 0)
    def _():
        for t in range(n_slots):
            factor = live_factor(slot_ref, t)
            for grp in range(groups):
                for i in range(edge):
                    row = field[t, i, :, grp * LANES : (grp + 1) * LANES].astype(F32)
                    first = t * area + i * edge
                    cells[grp, first : first + edge] = row * factor
        side[zero_at] = jnp.zeros(side.shape[1:], F32)
        corner[...] = jnp.zeros_like(corner)
        received_records(recv, side, corner, cap)
        own_records(cells, side, corner, base, edge, n_slots)
        spread_taps(taps, kernel_ref)
        reduce_sum[...] = jnp.zeros_like(reduce_sum)
        expand_sum[...] = jnp.zeros_like(expand_sum)

    padded = padded_out.at[0]
    for grp in range(groups):
        for i in range(edge):
            first = pl.multiple_of(s * area + i * edge, 8)
            padded[grp, RIM + i, COL0 : COL0 + edge] = cells[grp, pl.ds(first, edge)]
    place_rim(padded, side, corner, side_sources, corner_sources, s, zero_at, edge)

    def one_group(grp, carry):
        def emit(blk, row, total):
            own = mixed_own[0, grp, row, 8 * blk : 8 * blk + 8]
            first = row * edge + 8 * blk
            mixed[grp, first : first + 8] = own if total is None else own + total

        conv_group(padded, taps, grp, edge, "rim", False, emit)
        return carry

    lax.fori_loop(0, groups, one_group, 0)

    factor = live_factor(slot_ref, s)
    parts = [mixed[grp] for grp in range(groups)]
    mean = sum(jnp.sum(part, axis=1, keepdims=True) for part in parts) * (1.0 / channels)
    parts = [part - mean for part in parts]
    var = sum(jnp.sum(part * part, axis=1, keepdims=True) for part in parts) * (1.0 / channels)
    scale = lax.rsqrt(var + LN_EPS)
    unit = jnp.concatenate([part * scale for part in parts], axis=1)
    unit_ref[...] = unit
    normed = unit.astype(BF16)
    cot = (cotangent[...].astype(F32) * factor).astype(BF16)
    update = None
    grad_norm = None
    for n in range(0, hidden, 256):
        pre = mxu(normed, expand[:, n : n + 256], 1, 0)
        act, slope = gelu_parts(pre)
        act = act.astype(BF16)
        grad_pre = (grad_act_ref[:, n : n + 256] * slope).astype(BF16)
        term = mxu(act, reduce[n : n + 256], 1, 0)
        update = term if update is None else update + term
        reduce_sum[:, n : n + 256] += mxu(cot, act, 0, 0)
        expand_sum[n // 256] += mxu(normed, grad_pre, 0, 0)
        term = mxu(grad_pre, expand[:, n : n + 256], 1, 1)
        grad_norm = term if grad_norm is None else grad_norm + term
    at = pl.ds(pl.multiple_of(s * area, 8), area)
    for grp in range(groups):
        lanes = slice(grp * LANES, (grp + 1) * LANES)
        out[:, lanes] = ((cells[grp, at] + update[:, lanes]) * factor).astype(BF16)

    unit = unit_ref[...]
    mean = jnp.sum(grad_norm, axis=1, keepdims=True) * (1.0 / channels)
    along = jnp.sum(grad_norm * unit, axis=1, keepdims=True) * (1.0 / channels)
    grad = (scale * (grad_norm - mean - unit * along)).astype(BF16)
    grad_out[...] = grad
    for grp in range(groups):
        cells[grp, at] = grad[:, grp * LANES : (grp + 1) * LANES].astype(F32)

    @pl.when(s == slots - 1)
    def _():
        weights_out[:hidden] = jnp.transpose(reduce_sum[...]).astype(BF16)
        for n in range(hidden // 256):
            first = hidden + n * channels
            weights_out[first : first + channels] = expand_sum[n].astype(BF16)
        own_records(cells, side, corner, base, edge, n_slots)
        send_records(send, side, corner, side_sends, corner_sends, zero_at, base)


def fill_padded(padded, grad_ref, edge):
    for grp in range(padded.shape[0]):
        for i in range(edge):
            row = grad_ref[i * edge : (i + 1) * edge, grp * LANES : (grp + 1) * LANES]
            padded[grp, RIM + i, COL0 : COL0 + edge] = row.astype(F32)


def kernel_grad_body(padded_field, grad_ref, kernel_out, padded, sums, *, edge):
    s = pl.program_id(0)
    groups = padded.shape[0]

    @pl.when(s == 0)
    def _():
        sums[...] = jnp.zeros_like(sums)

    fill_padded(padded, grad_ref, edge)

    def one_group(grp, carry):
        kernel_grad_group(padded_field, padded, sums, grp, edge)
        return carry

    lax.fori_loop(0, groups, one_group, 0)

    @pl.when(s == pl.num_programs(0) - 1)
    def _():
        for grp in range(groups):
            lanes = slice(grp * LANES, (grp + 1) * LANES)
            rows = jnp.sum(sums[grp], axis=1)
            empty = jnp.zeros((kernel_out.shape[0] - TAPS, LANES), F32)
            kernel_out[:, lanes] = jnp.concatenate([rows, empty], axis=0).astype(BF16)


def final_body(
    slot_ref,
    side_sources,
    corner_sources,
    recv,
    grad_ref,
    cotangent,
    kernel_ref,
    *rest,
    edge,
    cap,
    first_slot,
):
    out, cells_out, side, corner, cells, padded, taps = rest[-7:]
    step = pl.program_id(0)
    s = step + first_slot
    groups = taps.shape[0]
    area = edge * edge
    n_slots = grad_ref.shape[0] // area
    base = recv.shape[0] * cap
    zero_at = base + 4 * n_slots

    @pl.when(step == 0)
    def _():
        for grp in range(groups):
            cells[grp] = grad_ref[:, grp * LANES : (grp + 1) * LANES].astype(F32)
        side[zero_at] = jnp.zeros(side.shape[1:], F32)
        corner[zero_at] = jnp.zeros(corner.shape[1:], F32)
        received_records(recv, side, corner, cap)
        own_records(cells, side, corner, base, edge, n_slots)
        spread_taps(taps, kernel_ref)

    for grp in range(groups):
        for i in range(edge):
            first = pl.multiple_of(s * area + i * edge, 8)
            padded[grp, RIM + i, COL0 : COL0 + edge] = cells[grp, pl.ds(first, edge)]
    place_rim(padded, side, corner, side_sources, corner_sources, s, zero_at, edge)
    factor = live_factor(slot_ref, s)

    def one_group(grp, carry):
        def emit(blk, row, total):
            first = row * edge + 8 * blk
            cells_out[grp, first : first + 8] = total

        conv_group(padded, taps, grp, edge, "all", True, emit)
        return carry

    lax.fori_loop(0, groups, one_group, 0)
    for grp in range(groups):
        lanes = slice(grp * LANES, (grp + 1) * LANES)
        total = cotangent[:, lanes].astype(F32) + cells_out[grp]
        out[:, lanes] = (total * factor).astype(BF16)


def weights_body(device, *refs, hidden, factor):
    blocks, (kernel_out, expand_out, reduce_out, rows) = refs[:-4], refs[-4:]
    channels = reduce_out.shape[1]
    part = 2 * hidden // len(blocks)
    kernel_sum = None
    for at, block in enumerate(blocks):
        pairs = len(blocks) // 2
        holder = device[0] if at < pairs else device[0] ^ 1
        source = lax.rem(holder - 2 * (at % pairs) + len(blocks), len(blocks))
        first = pl.multiple_of(source * part, 8)
        rows[pl.ds(first, part)] = block[:part].astype(F32) * factor
        kernel = block[part:].astype(F32)
        kernel_sum = kernel if kernel_sum is None else kernel_sum + kernel
    kernel_out[...] = kernel_sum[:TAPS] * factor
    reduce_out[...] = rows[:hidden]
    for n in range(hidden // 256):
        first = hidden + n * channels
        expand_out[:, n * 256 : (n + 1) * 256] = rows[first : first + channels]


def call(body, grid, ins, outs, scratch, flops=0, moved=0, aliases=None, limit=VMEM_LIMIT):
    in_specs = []
    for array, block, index in ins:
        if block is None:
            in_specs.append(pl.BlockSpec(memory_space=index))
        else:
            in_specs.append(pl.BlockSpec(block, index))
    return pl.pallas_call(
        body,
        grid=grid,
        in_specs=in_specs,
        out_specs=[pl.BlockSpec(block, index) for _, _, block, index in outs],
        out_shape=[jax.ShapeDtypeStruct(shape, dtype) for shape, dtype, _, _ in outs],
        scratch_shapes=scratch,
        input_output_aliases=aliases or {},
        compiler_params=pltpu.CompilerParams(vmem_limit_bytes=limit),
        cost_estimate=pl.CostEstimate(flops=flops, bytes_accessed=moved, transcendentals=0),
    )(*[array for array, _, _ in ins])


def whole(array):
    rank = array.ndim
    return (array, array.shape, lambda s: (0,) * rank)


def swap(blocks, axis):
    return lax.all_to_all(blocks, axis, split_axis=0, concat_axis=0, tiled=True)


def spread_blocks(blocks, axis):
    size = blocks.shape[0]
    me = lax.axis_index(axis)
    take = lambda at: lax.dynamic_index_in_dim(blocks, at, 0, keepdims=False)
    parts = [take(me)]
    for step in range(1, size):
        perm = [(i, (i + step) % size) for i in range(size)]
        parts.append(lax.ppermute(take((me + step) % size), axis, perm))
    return parts


def gather_blocks(block, axis):
    size = lax.axis_size(axis)
    swap_pair = [(i, i ^ 1) for i in range(size)]
    parts = [block]
    for step in range(2, size, 2):
        perm = [(i, (i + step) % size) for i in range(size)]
        parts.append(lax.ppermute(block, axis, perm))
    passed = [lax.ppermute(part, axis, swap_pair) for part in parts]
    return parts + passed


def on_device(
    ocean_fields,
    slot_tiles,
    side_sources,
    corner_sources,
    side_sends,
    corner_sends,
    depth_kernel,
    expand_weight,
    reduce_weight,
    field_cotangent,
):
    slots, edge, _, channels = ocean_fields.shape
    hidden = expand_weight.shape[1]
    tiles = lax.axis_size("tile")
    basins = lax.axis_size("basin")
    cap = side_sends.shape[2]
    groups = channels // LANES
    area = edge * edge
    cells = slots * area
    n_side = RIM * edge
    n_corner = 16
    send_rows = cap * (n_side + n_corner)
    table = tiles * cap + 4 * slots + 1
    wide = edge + 2 * COL0
    tall = edge + 2 * RIM

    cot_rows = field_cotangent.reshape(cells, channels)
    side_sends = jnp.transpose(side_sends.reshape(tiles, cap))
    corner_sends = jnp.transpose(corner_sends.reshape(tiles, cap))
    scalar = lambda array: (array, None, pltpu.SMEM)
    placed = lambda array: (array, None, pltpu.VMEM)
    by_slot = lambda array, width: (array, (area, width), lambda s: (s, 0))
    taps = pltpu.VMEM((groups, TAPS, 8, LANES), F32)
    cell_scratch = pltpu.VMEM((groups, cells, LANES), F32)
    padded_scratch = pltpu.VMEM((groups, tall, wide, LANES), F32)
    own_side = pltpu.VMEM((4 * slots + 1, groups, n_side, LANES), F32)
    own_corner = pltpu.VMEM((4 * slots + 1, groups, n_corner, LANES), F32)
    all_side = pltpu.VMEM((table, groups, n_side, LANES), F32)
    all_corner = pltpu.VMEM((table, groups, n_corner, LANES), F32)
    send_out = ((tiles, send_rows, channels), BF16, (tiles, send_rows, channels), lambda s: (0, 0, 0))
    tile_block = (1, groups, edge, edge, LANES)
    tile_out = ((slots,) + tile_block[1:], F32, tile_block, lambda s: (s, 0, 0, 0, 0))
    kernel_rows = tiles * 8 * -(-TAPS // (8 * tiles))
    mlp_flops = 6 * cells * channels * hidden
    field_bytes = cells * channels * 4

    (send,) = call(
        functools.partial(pack_body, edge=edge),
        (1,),
        [scalar(slot_tiles), scalar(side_sends), scalar(corner_sends), whole(ocean_fields)],
        [send_out],
        [cell_scratch, own_side, own_corner],
        moved=field_bytes,
    )
    recv = swap(send, "tile")
    mixed_own, grad_act = call(
        functools.partial(own_body, edge=edge),
        (slots,),
        [
            scalar(slot_tiles),
            (ocean_fields, (1, edge, edge, channels), lambda s: (s, 0, 0, 0)),
            whole(depth_kernel),
            by_slot(cot_rows, channels),
            whole(reduce_weight),
        ],
        [tile_out, ((cells, hidden), F32, (area, hidden), lambda s: (s, 0))],
        [padded_scratch, taps],
        flops=mlp_flops,
        moved=6 * field_bytes,
    )
    next_rows, padded, grad_rows, weights, send = call(
        functools.partial(mlp_body, edge=edge, cap=cap),
        (slots,),
        [
            scalar(slot_tiles),
            scalar(side_sources),
            scalar(corner_sources),
            scalar(side_sends),
            scalar(corner_sends),
            placed(recv),
            whole(ocean_fields),
            (mixed_own, tile_block, lambda s: (s, 0, 0, 0, 0)),
            by_slot(grad_act, hidden),
            by_slot(cot_rows, channels),
            whole(depth_kernel),
            whole(expand_weight),
            whole(reduce_weight),
        ],
        [
            ((cells, channels), BF16, (area, channels), lambda s: (s, 0)),
            (
                (slots, groups, tall, wide, LANES),
                F32,
                (1, groups, tall, wide, LANES),
                lambda s: (s, 0, 0, 0, 0),
            ),
            ((cells, channels), BF16, (area, channels), lambda s: (s, 0)),
            ((2 * hidden, channels), BF16, (2 * hidden, channels), lambda s: (0, 0)),
            send_out,
        ],
        [
            all_side,
            all_corner,
            cell_scratch,
            taps,
            pltpu.VMEM((groups, area, LANES), F32),
            pltpu.VMEM((area, channels), F32),
            pltpu.VMEM((channels, hidden), F32),
            pltpu.VMEM((hidden // 256, channels, 256), F32),
        ],
        flops=2 * mlp_flops,
        moved=6 * field_bytes,
    )
    recv = swap(send, "tile")
    rows = 2 * hidden
    blocks = spread_blocks(weights.reshape(basins, rows // basins, channels), "basin")
    (kernel_part,) = call(
        functools.partial(kernel_grad_body, edge=edge),
        (slots,),
        [
            (padded, (1, groups, tall, wide, LANES), lambda s: (s, 0, 0, 0, 0)),
            by_slot(grad_rows, channels),
        ],
        [((kernel_rows, channels), BF16, (kernel_rows, channels), lambda s: (0, 0))],
        [padded_scratch, taps],
        flops=mlp_flops,
        moved=4 * field_bytes,
    )
    mine = sum(block.astype(F32) for block in blocks).astype(BF16)
    part = rows // basins // tiles
    mine = jnp.concatenate(
        [
            mine.reshape(tiles, part, channels),
            kernel_part.reshape(tiles, kernel_rows // tiles, channels),
        ],
        axis=1,
    )
    blocks = swap(mine, "tile")
    half = slots // 2
    device = lax.axis_index("basin").reshape(1)

    def final(first_slot, count, previous):
        rows_at = lambda s: (s + first_slot, 0)
        ins = [
            scalar(slot_tiles),
            scalar(side_sources),
            scalar(corner_sources),
            placed(recv),
            whole(grad_rows),
            (cot_rows, (area, channels), rows_at),
            whole(depth_kernel),
        ]
        if previous is not None:
            ins.append((previous, None, pl.ANY))
        (rows_out,) = call(
            functools.partial(final_body, edge=edge, cap=cap, first_slot=first_slot),
            (count,),
            ins,
            [((cells, channels), BF16, (area, channels), rows_at)],
            [
                pltpu.VMEM((groups, area, LANES), F32),
                all_side,
                all_corner,
                cell_scratch,
                padded_scratch,
                taps,
            ],
            flops=mlp_flops // 2,
            moved=3 * field_bytes,
            aliases=None if previous is None else {len(ins) - 1: 0},
        )
        return rows_out

    grad_field = final(0, half, None)
    mine = jnp.sum(blocks.astype(F32), axis=0).astype(BF16)
    blocks = swap(jnp.broadcast_to(mine[None], (tiles,) + mine.shape), "tile")
    mine = jnp.concatenate(
        [
            blocks[:, :part].reshape(rows // basins, channels),
            blocks[:, part:].reshape(kernel_rows, channels),
        ],
        axis=0,
    )
    blocks = gather_blocks(mine, "basin")
    grad_field = final(half, slots - half, grad_field)
    factor = 1.0 / math.sqrt(basins * tiles * cells)
    kernel_total, expand_total, reduce_total = call(
        functools.partial(weights_body, hidden=hidden, factor=factor),
        (1,),
        [scalar(device)] + [placed(block) for block in blocks],
        [
            ((TAPS, channels), F32, (TAPS, channels), lambda s: (0, 0)),
            ((channels, hidden), F32, (channels, hidden), lambda s: (0, 0)),
            ((hidden, channels), F32, (hidden, channels), lambda s: (0, 0)),
        ],
        [pltpu.VMEM((rows, channels), F32)],
        moved=6 * hidden * channels * 2,
        limit=VMEM_LIMIT // 4,
    )
    shape = ocean_fields.shape
    return (
        next_rows.reshape(shape),
        grad_field.reshape(shape),
        kernel_total,
        expand_total,
        reduce_total,
    )


def solution(mesh):
    split = ("basin", "tile")
    field = P(split, None, None, None)
    table = P(split, None, None)
    pair = P(split, None)

    return jax.shard_map(
        on_device,
        mesh=mesh,
        in_specs=(field, P(split), pair, pair, table, table, P(), P(), P(), field),
        out_specs=(field, field, P(), P(), P()),
        check_vma=False,
    )
```

```python
import functools
import math

import jax
import jax.numpy as jnp
from jax import lax
from jax.experimental import pallas as pl
from jax.experimental.pallas import tpu as pltpu
from jax.sharding import PartitionSpec as P


KERNEL = 7
TAPS = KERNEL * KERNEL
RIM = 3
LANES = 128
COL0 = 8
LN_EPS = 1e-06
F32 = jnp.float32
BF16 = jnp.bfloat16
VMEM_LIMIT = 60 * 1024 * 1024


def mxu(lhs, rhs, lhs_dim, rhs_dim):
    return lax.dot_general(
        lhs, rhs, (((lhs_dim,), (rhs_dim,)), ((), ())), preferred_element_type=F32
    )


def gelu_parts(pre):
    cdf = 0.5 * (1.0 + lax.erf(pre * (1.0 / math.sqrt(2.0))))
    density = jnp.exp(-0.5 * pre * pre) * (1.0 / math.sqrt(2.0 * math.pi))
    return pre * cdf, cdf + pre * density


def live_factor(slot_ref, slot):
    return jnp.where(slot_ref[slot] >= 0, 1.0, 0.0).astype(F32)


def own_records(cells, side, corner, base, edge, slots):
    area = edge * edge
    rim_rows = RIM * edge
    far = edge - RIM
    for grp in range(cells.shape[0]):
        for s in range(slots):
            at = base + 4 * s
            start = s * area
            side[at, grp] = cells[grp, start : start + rim_rows]
            side[at + 1, grp] = cells[grp, start + area - rim_rows : start + area]
            for c in range(RIM):
                rows = slice(c * edge, (c + 1) * edge)
                side[at + 2, grp, rows] = cells[grp, pl.ds(start + c, edge, stride=edge)]
                side[at + 3, grp, rows] = cells[grp, pl.ds(start + far + c, edge, stride=edge)]
            for e in range(4):
                row0 = far if e // 2 else 0
                col0 = far if e % 2 else 0
                for r in range(RIM):
                    first = start + (row0 + r) * edge + col0
                    corner[at + e, grp, RIM * r : RIM * r + RIM] = cells[grp, first : first + RIM]


def send_records(send, side, corner, side_sends, corner_sends, zero_at, base=0):
    peers = send.shape[0]
    groups = side.shape[1]
    cap = side_sends.shape[0]

    def one_peer(p, carry):
        for grp in range(groups):
            pieces = []
            for table, sends in ((side, side_sends), (corner, corner_sends)):
                for k in range(cap):
                    code = sends[k, p]
                    pieces.append(table[jnp.where(code < 0, zero_at, code + base), grp])
            block = jnp.concatenate(pieces, axis=0)
            send[p, :, grp * LANES : (grp + 1) * LANES] = block.astype(BF16)
        return carry

    lax.fori_loop(0, peers, one_peer, 0)


def received_records(recv, side, corner, cap):
    groups = side.shape[1]
    n_side = side.shape[2]
    n_corner = corner.shape[2]

    def one_peer(p, carry):
        for grp in range(groups):
            block = recv[p, :, grp * LANES : (grp + 1) * LANES].astype(F32)
            for k in range(cap):
                side[p * cap + k, grp] = block[k * n_side : (k + 1) * n_side]
                first = cap * n_side + k * n_corner
                corner[p * cap + k, grp] = block[first : first + n_corner]
        return carry

    lax.fori_loop(0, recv.shape[0], one_peer, 0)


def place_rim(padded, side, corner, side_sources, corner_sources, slot, zero_at, edge):
    for e in range(4):
        code = side_sources[slot, e]
        at = jnp.where(code < 0, zero_at, code)
        for grp in range(side.shape[1]):
            for c in range(RIM):
                piece = side[at, grp, c * edge : (c + 1) * edge]
                if e < 2:
                    row = c if e == 0 else RIM + edge + c
                    padded[grp, row, COL0 : COL0 + edge] = piece
                else:
                    col = COL0 - RIM + c if e == 2 else COL0 + edge + c
                    padded[grp, RIM : RIM + edge, col] = piece
        code = corner_sources[slot, e]
        at = jnp.where(code < 0, zero_at, code)
        row0 = RIM + edge if e // 2 else 0
        col0 = COL0 + edge if e % 2 else COL0 - RIM
        for grp in range(side.shape[1]):
            for r in range(RIM):
                padded[grp, row0 + r, col0 : col0 + RIM] = corner[
                    at, grp, RIM * r : RIM * r + RIM
                ]


def spread_taps(taps, kernel_ref):
    for grp in range(taps.shape[0]):
        for t in range(TAPS):
            row = kernel_ref[t : t + 1, grp * LANES : (grp + 1) * LANES].astype(F32)
            taps[grp, t] = jnp.broadcast_to(row, taps.shape[2:])


def conv_group(padded, taps, grp, edge, part, flipped, emit):
    blocks = edge // 8
    lane = lax.broadcasted_iota(jnp.int32, (8, LANES), 0)
    for blk in range(blocks):
        acc = [None] * edge
        for b in range(KERNEL):
            west = part == "rim" and blk == 0 and b < RIM
            east = part == "rim" and blk == blocks - 1 and b > RIM
            weights = []
            for a in range(KERNEL):
                t = a * KERNEL + b
                weights.append(taps[grp, TAPS - 1 - t if flipped else t])
            for r in range(edge + 2 * RIM):
                inner = RIM <= r < RIM + edge
                if part == "own" and not inner:
                    continue
                if part == "rim" and inner and not (west or east):
                    continue
                first = COL0 - RIM + b + 8 * blk
                cells = padded[grp, r, first : first + 8]
                if part == "rim" and inner:
                    keep = lane < RIM - b if west else lane >= 8 + RIM - b
                    cells = jnp.where(keep, cells, 0.0)
                for a in range(KERNEL):
                    row = r - a
                    if 0 <= row < edge:
                        term = cells * weights[a]
                        acc[row] = term if acc[row] is None else acc[row] + term
        for row in range(edge):
            emit(blk, row, acc[row])


def kernel_grad_group(padded, grad, sums, grp, edge):
    for b in range(KERNEL):
        acc = [None] * KERNEL
        for blk in range(edge // 8):
            rows = [grad[grp, RIM + i, COL0 + 8 * blk : COL0 + 8 * blk + 8] for i in range(edge)]
            for r in range(edge + 2 * RIM):
                first = COL0 - RIM + b + 8 * blk
                cells = padded[0, grp, r, first : first + 8]
                for a in range(KERNEL):
                    if 0 <= r - a < edge:
                        term = rows[r - a] * cells
                        acc[a] = term if acc[a] is None else acc[a] + term
        for a in range(KERNEL):
            sums[grp, a * KERNEL + b] += acc[a]


def pack_body(slot_ref, side_sends, corner_sends, field, send, cells, side, corner, *, edge):
    slots = field.shape[0]
    own = 4 * slots
    area = edge * edge
    for s in range(slots):
        factor = live_factor(slot_ref, s)
        for grp in range(cells.shape[0]):
            for i in list(range(edge)):
                row = field[s, i, :, grp * LANES : (grp + 1) * LANES].astype(F32)
                first = s * area + i * edge
                cells[grp, first : first + edge] = row * factor
    side[own] = jnp.zeros(side.shape[1:], F32)
    corner[...] = jnp.zeros_like(corner)
    own_records(cells, side, corner, 0, edge, slots)
    send_records(send, side, corner, side_sends, corner_sends, own)


def own_body(
    slot_ref, field, kernel_ref, cotangent, reduce, mixed, grad_act, padded, taps, *, edge
):
    s = pl.program_id(0)
    groups = padded.shape[0]
    share = cotangent.shape[0] // groups

    @pl.when(s == 0)
    def _():
        padded[...] = jnp.zeros_like(padded)
        spread_taps(taps, kernel_ref)

    factor = live_factor(slot_ref, s)
    for grp in range(groups):
        for i in range(edge):
            row = field[0, i, :, grp * LANES : (grp + 1) * LANES].astype(F32)
            padded[grp, RIM + i, COL0 : COL0 + edge] = row * factor

    def one_group(grp, carry):
        def emit(blk, row, total):
            mixed[0, grp, row, 8 * blk : 8 * blk + 8] = total

        rows = pl.ds(pl.multiple_of(grp * share, 16), share)
        cot = (cotangent[rows].astype(F32) * factor).astype(BF16)
        for n in range(0, reduce.shape[0], 256):
            grad_act[rows, n : n + 256] = mxu(cot, reduce[n : n + 256], 1, 1)
        conv_group(padded, taps, grp, edge, "own", False, emit)
        return carry

    lax.fori_loop(0, groups, one_group, 0)


def mlp_body(
    slot_ref,
    side_sources,
    corner_sources,
    side_sends,
    corner_sends,
    recv,
    field,
    mixed_own,
    grad_act_ref,
    cotangent,
    kernel_ref,
    expand,
    reduce,
    out,
    padded_out,
    grad_out,
    weights_out,
    send,
    side,
    corner,
    cells,
    taps,
    mixed,
    unit_ref,
    reduce_sum,
    expand_sum,
    *,
    edge,
    cap,
):
    s = pl.program_id(0)
    slots = pl.num_programs(0)
    groups = taps.shape[0]
    area = edge * edge
    n_slots = field.shape[0]
    base = recv.shape[0] * cap
    zero_at = base + 4 * n_slots
    hidden = expand.shape[1]
    channels = groups * LANES

    @pl.when(s == 0)
    def _():
        for t in range(n_slots):
            factor = live_factor(slot_ref, t)
            for grp in range(groups):
                for i in range(edge):
                    row = field[t, i, :, grp * LANES : (grp + 1) * LANES].astype(F32)
                    first = t * area + i * edge
                    cells[grp, first : first + edge] = row * factor
        side[zero_at] = jnp.zeros(side.shape[1:], F32)
        corner[...] = jnp.zeros_like(corner)
        received_records(recv, side, corner, cap)
        own_records(cells, side, corner, base, edge, n_slots)
        spread_taps(taps, kernel_ref)
        reduce_sum[...] = jnp.zeros_like(reduce_sum)
        expand_sum[...] = jnp.zeros_like(expand_sum)

    padded = padded_out.at[0]
    for grp in range(groups):
        for i in range(edge):
            first = pl.multiple_of(s * area + i * edge, 8)
            padded[grp, RIM + i, COL0 : COL0 + edge] = cells[grp, pl.ds(first, edge)]
    place_rim(padded, side, corner, side_sources, corner_sources, s, zero_at, edge)

    def one_group(grp, carry):
        def emit(blk, row, total):
            own = mixed_own[0, grp, row, 8 * blk : 8 * blk + 8]
            first = row * edge + 8 * blk
            mixed[grp, first : first + 8] = own if total is None else own + total

        conv_group(padded, taps, grp, edge, "rim", False, emit)
        return carry

    lax.fori_loop(0, groups, one_group, 0)

    factor = live_factor(slot_ref, s)
    parts = [mixed[grp] for grp in range(groups)]
    mean = sum(jnp.sum(part, axis=1, keepdims=True) for part in parts) * (1.0 / channels)
    parts = [part - mean for part in parts]
    var = sum(jnp.sum(part * part, axis=1, keepdims=True) for part in parts) * (1.0 / channels)
    scale = lax.rsqrt(var + LN_EPS)
    unit = jnp.concatenate([part * scale for part in parts], axis=1)
    unit_ref[...] = unit
    normed = unit.astype(BF16)
    cot = (cotangent[...].astype(F32) * factor).astype(BF16)
    update = None
    grad_norm = None
    for n in range(0, hidden, 256):
        pre = mxu(normed, expand[:, n : n + 256], 1, 0)
        act, slope = gelu_parts(pre)
        act = act.astype(BF16)
        grad_pre = (grad_act_ref[:, n : n + 256] * slope).astype(BF16)
        term = mxu(act, reduce[n : n + 256], 1, 0)
        update = term if update is None else update + term
        reduce_sum[:, n : n + 256] += mxu(cot, act, 0, 0)
        expand_sum[n // 256] += mxu(normed, grad_pre, 0, 0)
        term = mxu(grad_pre, expand[:, n : n + 256], 1, 1)
        grad_norm = term if grad_norm is None else grad_norm + term
    at = pl.ds(pl.multiple_of(s * area, 8), area)
    for grp in range(groups):
        lanes = slice(grp * LANES, (grp + 1) * LANES)
        out[:, lanes] = ((cells[grp, at] + update[:, lanes]) * factor).astype(BF16)

    unit = unit_ref[...]
    mean = jnp.sum(grad_norm, axis=1, keepdims=True) * (1.0 / channels)
    along = jnp.sum(grad_norm * unit, axis=1, keepdims=True) * (1.0 / channels)
    grad = (scale * (grad_norm - mean - unit * along)).astype(BF16)
    grad_out[...] = grad
    for grp in range(groups):
        cells[grp, at] = grad[:, grp * LANES : (grp + 1) * LANES].astype(F32)

    @pl.when(s == slots - 1)
    def _():
        weights_out[:hidden] = jnp.transpose(reduce_sum[...]).astype(BF16)
        for n in range(hidden // 256):
            first = hidden + n * channels
            weights_out[first : first + channels] = expand_sum[n].astype(BF16)
        own_records(cells, side, corner, base, edge, n_slots)
        send_records(send, side, corner, side_sends, corner_sends, zero_at, base)


def fill_padded(padded, grad_ref, edge):
    for grp in range(padded.shape[0]):
        for i in range(edge):
            row = grad_ref[i * edge : (i + 1) * edge, grp * LANES : (grp + 1) * LANES]
            padded[grp, RIM + i, COL0 : COL0 + edge] = row.astype(F32)


def kernel_grad_body(padded_field, grad_ref, kernel_out, padded, sums, *, edge):
    s = pl.program_id(0)
    groups = padded.shape[0]

    @pl.when(s == 0)
    def _():
        sums[...] = jnp.zeros_like(sums)

    fill_padded(padded, grad_ref, edge)

    def one_group(grp, carry):
        kernel_grad_group(padded_field, padded, sums, grp, edge)
        return carry

    lax.fori_loop(0, groups, one_group, 0)

    @pl.when(s == pl.num_programs(0) - 1)
    def _():
        for grp in range(groups):
            lanes = slice(grp * LANES, (grp + 1) * LANES)
            rows = jnp.sum(sums[grp], axis=1)
            empty = jnp.zeros((kernel_out.shape[0] - TAPS, LANES), F32)
            kernel_out[:, lanes] = jnp.concatenate([rows, empty], axis=0).astype(BF16)


def final_body(
    slot_ref,
    side_sources,
    corner_sources,
    recv,
    grad_ref,
    cotangent,
    kernel_ref,
    *rest,
    edge,
    cap,
    first_slot,
):
    out, cells_out, side, corner, cells, padded, taps = rest[-7:]
    step = pl.program_id(0)
    s = step + first_slot
    groups = taps.shape[0]
    area = edge * edge
    n_slots = grad_ref.shape[0] // area
    base = recv.shape[0] * cap
    zero_at = base + 4 * n_slots

    @pl.when(step == 0)
    def _():
        for grp in range(groups):
            cells[grp, : n_slots * area] = grad_ref[:, grp * LANES : (grp + 1) * LANES].astype(F32)
        side[zero_at] = jnp.zeros(side.shape[1:], F32)
        corner[zero_at] = jnp.zeros(corner.shape[1:], F32)
        received_records(recv, side, corner, cap)
        own_records(cells, side, corner, base, edge, n_slots)
        spread_taps(taps, kernel_ref)

    for grp in range(groups):
        for i in range(edge):
            first = pl.multiple_of(s * area + i * edge, 8)
            padded[grp, RIM + i, COL0 : COL0 + edge] = cells[grp, pl.ds(first, edge)]
    place_rim(padded, side, corner, side_sources, corner_sources, s, zero_at, edge)
    factor = live_factor(slot_ref, s)

    def one_group(grp, carry):
        def emit(blk, row, total):
            first = row * edge + 8 * blk
            cells_out[grp, first : first + 8] = total

        conv_group(padded, taps, grp, edge, "all", True, emit)
        return carry

    lax.fori_loop(0, groups, one_group, 0)
    for grp in range(groups):
        lanes = slice(grp * LANES, (grp + 1) * LANES)
        total = cotangent[:, lanes].astype(F32) + cells_out[grp]
        out[:, lanes] = (total * factor).astype(BF16)


def weights_body(device, *refs, hidden, factor):
    blocks, (kernel_out, expand_out, reduce_out, rows) = refs[:-4], refs[-4:]
    channels = reduce_out.shape[1]
    part = 2 * hidden // len(blocks)
    kernel_sum = None
    for at, block in enumerate(blocks):
        pairs = len(blocks) // 2
        holder = device[0] if at < pairs else device[0] ^ 1
        source = lax.rem(holder - 2 * (at % pairs) + len(blocks), len(blocks))
        first = pl.multiple_of(source * part, 8)
        rows[pl.ds(first, part)] = block[:part].astype(F32) * factor
        kernel = block[part:].astype(F32)
        kernel_sum = kernel if kernel_sum is None else kernel_sum + kernel
    kernel_out[...] = kernel_sum[:TAPS] * factor
    reduce_out[...] = rows[:hidden]
    for n in range(hidden // 256):
        first = hidden + n * channels
        expand_out[:, n * 256 : (n + 1) * 256] = rows[first : first + channels]


def call(body, grid, ins, outs, scratch, flops=0, moved=0, aliases=None, limit=VMEM_LIMIT):
    in_specs = []
    for array, block, index in ins:
        if block is None:
            in_specs.append(pl.BlockSpec(memory_space=index))
        else:
            in_specs.append(pl.BlockSpec(block, index))
    return pl.pallas_call(
        body,
        grid=grid,
        in_specs=in_specs,
        out_specs=[pl.BlockSpec(block, index) for _, _, block, index in outs],
        out_shape=[jax.ShapeDtypeStruct(shape, dtype) for shape, dtype, _, _ in outs],
        scratch_shapes=scratch,
        input_output_aliases=aliases or {},
        compiler_params=pltpu.CompilerParams(vmem_limit_bytes=limit),
        cost_estimate=pl.CostEstimate(flops=flops, bytes_accessed=moved, transcendentals=0),
    )(*[array for array, _, _ in ins])


def whole(array):
    rank = array.ndim
    return (array, array.shape, lambda s: (0,) * rank)


def swap(blocks, axis):
    return lax.all_to_all(blocks, axis, split_axis=0, concat_axis=0, tiled=True)


def spread_blocks(blocks, axis):
    size = blocks.shape[0]
    me = lax.axis_index(axis)
    take = lambda at: lax.dynamic_index_in_dim(blocks, at, 0, keepdims=False)
    parts = [take(me)]
    for step in range(1, size):
        perm = [(i, (i + step) % size) for i in range(size)]
        parts.append(lax.ppermute(take((me + step) % size), axis, perm))
    return parts


def gather_blocks(block, axis):
    size = lax.axis_size(axis)
    swap_pair = [(i, i ^ 1) for i in range(size)]
    parts = [block]
    for step in range(2, size, 2):
        perm = [(i, (i + step) % size) for i in range(size)]
        parts.append(lax.ppermute(block, axis, perm))
    passed = [lax.ppermute(part, axis, swap_pair) for part in parts]
    return parts + passed


def on_device(
    ocean_fields,
    slot_tiles,
    side_sources,
    corner_sources,
    side_sends,
    corner_sends,
    depth_kernel,
    expand_weight,
    reduce_weight,
    field_cotangent,
):
    slots, edge, _, channels = ocean_fields.shape
    hidden = expand_weight.shape[1]
    tiles = lax.axis_size("tile")
    basins = lax.axis_size("basin")
    cap = side_sends.shape[2]
    groups = channels // LANES
    area = edge * edge
    cells = slots * area
    n_side = RIM * edge
    n_corner = 16
    send_rows = cap * (n_side + n_corner)
    table = tiles * cap + 4 * slots + 1
    wide = edge + 2 * COL0
    tall = edge + 2 * RIM

    cot_rows = field_cotangent.reshape(cells, channels)
    side_sends = jnp.transpose(side_sends.reshape(tiles, cap))
    corner_sends = jnp.transpose(corner_sends.reshape(tiles, cap))
    scalar = lambda array: (array, None, pltpu.SMEM)
    placed = lambda array: (array, None, pltpu.VMEM)
    by_slot = lambda array, width: (array, (area, width), lambda s: (s, 0))
    taps = pltpu.VMEM((groups, TAPS, 8, LANES), F32)
    cell_scratch = pltpu.VMEM((groups, cells + 8, LANES), F32)
    padded_scratch = pltpu.VMEM((groups, tall, wide, LANES), F32)
    own_side = pltpu.VMEM((4 * slots + 1, groups, n_side, LANES), F32)
    own_corner = pltpu.VMEM((4 * slots + 1, groups, n_corner, LANES), F32)
    all_side = pltpu.VMEM((table, groups, n_side, LANES), F32)
    all_corner = pltpu.VMEM((table, groups, n_corner, LANES), F32)
    send_out = ((tiles, send_rows, channels), BF16, (tiles, send_rows, channels), lambda s: (0, 0, 0))
    tile_block = (1, groups, edge, edge, LANES)
    tile_out = ((slots,) + tile_block[1:], F32, tile_block, lambda s: (s, 0, 0, 0, 0))
    kernel_rows = tiles * 8 * -(-TAPS // (8 * tiles))
    mlp_flops = 6 * cells * channels * hidden
    field_bytes = cells * channels * 4

    (send,) = call(
        functools.partial(pack_body, edge=edge),
        (1,),
        [scalar(slot_tiles), scalar(side_sends), scalar(corner_sends), whole(ocean_fields)],
        [send_out],
        [cell_scratch, own_side, own_corner],
        moved=field_bytes,
    )
    recv = swap(send, "tile")
    mixed_own, grad_act = call(
        functools.partial(own_body, edge=edge),
        (slots,),
        [
            scalar(slot_tiles),
            (ocean_fields, (1, edge, edge, channels), lambda s: (s, 0, 0, 0)),
            whole(depth_kernel),
            by_slot(cot_rows, channels),
            whole(reduce_weight),
        ],
        [tile_out, ((cells, hidden), F32, (area, hidden), lambda s: (s, 0))],
        [padded_scratch, taps],
        flops=mlp_flops,
        moved=6 * field_bytes,
    )
    next_rows, padded, grad_rows, weights, send = call(
        functools.partial(mlp_body, edge=edge, cap=cap),
        (slots,),
        [
            scalar(slot_tiles),
            scalar(side_sources),
            scalar(corner_sources),
            scalar(side_sends),
            scalar(corner_sends),
            placed(recv),
            whole(ocean_fields),
            (mixed_own, tile_block, lambda s: (s, 0, 0, 0, 0)),
            by_slot(grad_act, hidden),
            by_slot(cot_rows, channels),
            whole(depth_kernel),
            whole(expand_weight),
            whole(reduce_weight),
        ],
        [
            ((cells, channels), BF16, (area, channels), lambda s: (s, 0)),
            (
                (slots, groups, tall, wide, LANES),
                F32,
                (1, groups, tall, wide, LANES),
                lambda s: (s, 0, 0, 0, 0),
            ),
            ((cells, channels), BF16, (area, channels), lambda s: (s, 0)),
            ((2 * hidden, channels), BF16, (2 * hidden, channels), lambda s: (0, 0)),
            send_out,
        ],
        [
            all_side,
            all_corner,
            cell_scratch,
            taps,
            pltpu.VMEM((groups, area, LANES), F32),
            pltpu.VMEM((area, channels), F32),
            pltpu.VMEM((channels, hidden), F32),
            pltpu.VMEM((hidden // 256, channels, 256), F32),
        ],
        flops=2 * mlp_flops,
        moved=6 * field_bytes,
        limit=VMEM_LIMIT - 2 * 1024 * 1024,
    )
    recv = swap(send, "tile")
    rows = 2 * hidden
    blocks = spread_blocks(weights.reshape(basins, rows // basins, channels), "basin")
    (kernel_part,) = call(
        functools.partial(kernel_grad_body, edge=edge),
        (slots,),
        [
            (padded, (1, groups, tall, wide, LANES), lambda s: (s, 0, 0, 0, 0)),
            by_slot(grad_rows, channels),
        ],
        [((kernel_rows, channels), BF16, (kernel_rows, channels), lambda s: (0, 0))],
        [padded_scratch, taps],
        flops=mlp_flops,
        moved=4 * field_bytes,
    )
    mine = sum(block.astype(F32) for block in blocks).astype(BF16)
    part = rows // basins // tiles
    mine = jnp.concatenate(
        [
            mine.reshape(tiles, part, channels),
            kernel_part.reshape(tiles, kernel_rows // tiles, channels),
        ],
        axis=1,
    )
    blocks = swap(mine, "tile")
    half = slots // 2
    device = lax.axis_index("basin").reshape(1)

    def final(first_slot, count, previous):
        rows_at = lambda s: (s + first_slot, 0)
        ins = [
            scalar(slot_tiles),
            scalar(side_sources),
            scalar(corner_sources),
            placed(recv),
            whole(grad_rows),
            (cot_rows, (area, channels), rows_at),
            whole(depth_kernel),
        ]
        if previous is not None:
            ins.append((previous, None, pl.ANY))
        (rows_out,) = call(
            functools.partial(final_body, edge=edge, cap=cap, first_slot=first_slot),
            (count,),
            ins,
            [((cells, channels), BF16, (area, channels), rows_at)],
            [
                pltpu.VMEM((groups, area, LANES), F32),
                all_side,
                all_corner,
                cell_scratch,
                padded_scratch,
                taps,
            ],
            flops=mlp_flops // 2,
            moved=3 * field_bytes,
            aliases=None if previous is None else {len(ins) - 1: 0},
        )
        return rows_out

    grad_field = final(0, half, None)
    mine = jnp.sum(blocks.astype(F32), axis=0).astype(BF16)
    blocks = swap(jnp.broadcast_to(mine[None], (tiles,) + mine.shape), "tile")
    mine = jnp.concatenate(
        [
            blocks[:, :part].reshape(rows // basins, channels),
            blocks[:, part:].reshape(kernel_rows, channels),
        ],
        axis=0,
    )
    blocks = gather_blocks(mine, "basin")
    grad_field = final(half, slots - half, grad_field)
    factor = 1.0 / math.sqrt(basins * tiles * cells)
    kernel_total, expand_total, reduce_total = call(
        functools.partial(weights_body, hidden=hidden, factor=factor),
        (1,),
        [scalar(device)] + [placed(block) for block in blocks],
        [
            ((TAPS, channels), F32, (TAPS, channels), lambda s: (0, 0)),
            ((channels, hidden), F32, (channels, hidden), lambda s: (0, 0)),
            ((hidden, channels), F32, (hidden, channels), lambda s: (0, 0)),
        ],
        [pltpu.VMEM((rows, channels), F32)],
        moved=6 * hidden * channels * 2,
        limit=VMEM_LIMIT // 4,
    )
    shape = ocean_fields.shape
    return (
        next_rows.reshape(shape),
        grad_field.reshape(shape),
        kernel_total,
        expand_total,
        reduce_total,
    )


def solution(mesh):
    split = ("basin", "tile")
    field = P(split, None, None, None)
    table = P(split, None, None)
    pair = P(split, None)

    return jax.shard_map(
        on_device,
        mesh=mesh,
        in_specs=(field, P(split), pair, pair, table, table, P(), P(), P(), field),
        out_specs=(field, field, P(), P(), P()),
        check_vma=False,
    )
```
